512 devices in a mesh: seq: 32 (over x, z), head: 16 (over y, core).
Axes of the slice: x: 4, y: 8, z: 8, core: 2. Of those that a mesh axis runs over, the one named last changes fastest.
Arguments:
- query_rows: float32 [16384, 4096], P('seq', 'head'), may hold values from -128 to 128
- key_rows: float32 [16384, 4096], P('seq', 'head'), may hold values from -128 to 128
- value_rows: float32 [16384, 4096], P('seq', 'head'), may hold values from -6 to 6
- teacher_out: float32 [16384, 4096], P(('seq', 'head')), may hold values from -6 to 6
- query_map: float32 [16, 256, 256], P('head'), may hold values from -1 to 1
- key_map: float32 [16, 256, 256], P('head'), may hold values from -1 to 1
- block_map: int32 [32, 32], replicated, may hold values from 0 to 1023, as said below
Outputs:
- grad_query_map: float32 [16, 256, 256], P('head', 'seq')
- grad_key_map: float32 [16, 256, 256], P('head', 'seq')
The draws below stay inside these ranges and needn't reach their ends.
Inputs may be any that keep to these rules, and one draw needn't show every extreme that they name: `block_map`: row d lists, slot by slot, the sequence blocks whose teacher rows storage row group d holds (storage block d * 32 + j). Sequence block b belongs to owner b // 32. Every row names exactly one block of each owner, and every block appears exactly once in the table.
All inputs are finite; a program needn't handle non-finite values.
Results may differ from the reference program's by a relative error of at most 0.00035.
Values sent between devices are 32-bit elements; how exact they have to be, the bound alone decides.
No kernel may reach another device: no remote copies, remote signals or barrier semaphores. Data moves between devices by JAX's collectives and lax.ppermute only.
A program may use at most 128 MiB of HBM per device.

```python
import jax
import jax.numpy as jnp
from jax import lax

E = 256
HEADS = 16
FH = 256
TOK_DEV = 512
SEQ = 16384
OWNERS = 32
BLK = 16


def weights_for(key, which):
    return jax.random.normal(jax.random.fold_in(key, 11 + which), (HEADS, E, FH), jnp.float32) * E ** (-0.5)


def draw_rows(key, which):
    base_rows = jnp.clip(jax.random.normal(jax.random.fold_in(key, 21 + which), (SEQ, HEADS * E), jnp.float32), -6.0, 6.0)
    return base_rows


def draw_query_rows(key, part):
    return draw_rows(key, 0)


def draw_key_rows(key, part):
    return draw_rows(key, 1)


def draw_query_map(key, part):
    return weights_for(key, 0)


def draw_key_map(key, part):
    return weights_for(key, 1)


def draw_block_map(key, part):
    owner_keys = jax.random.split(jax.random.fold_in(key, 41), OWNERS)
    slot_keys = jax.random.split(jax.random.fold_in(key, 42), OWNERS)
    within_order = jax.vmap(lambda sub_key: jax.random.permutation(sub_key, OWNERS))(owner_keys)
    slot_owner = jax.vmap(lambda sub_key: jax.random.permutation(sub_key, OWNERS))(slot_keys)
    within_by_device = jnp.transpose(within_order)
    picked = jnp.take_along_axis(within_by_device, slot_owner, axis=1)
    return (slot_owner * OWNERS + picked).astype(jnp.int32)


def levels(key, extent, shards, least, largest):
    loudness = 1.0
    for position, blocks in shards:
        draws = jax.random.uniform(jax.random.fold_in(jax.random.fold_in(key, 6), position), (blocks,), jnp.float32, least / len(shards), largest / len(shards))
        loudness = loudness * jnp.repeat(jnp.exp(draws), extent[position] // blocks).reshape((-1,) + (1,) * (len(extent) - 1 - position))
    return loudness


def scatter_about(own_key, dims, scale, limit, cuts=(), kind=jnp.bfloat16):
    level = levels(own_key, dims, cuts, -0.22, 0.18) if cuts else 1.0
    values = jax.random.normal(own_key, dims, jnp.float32) * scale * level
    return jnp.minimum(jnp.maximum(values, -limit), limit).astype(kind)


def setup_inputs(seed: int = 0) -> dict:
    arg_keys = jax.random.split(jax.random.key(seed), 8)
    return {
        "query_rows": draw_query_rows(jax.random.fold_in(arg_keys[7], 71), 0),
        "key_rows": draw_key_rows(jax.random.fold_in(arg_keys[7], 71), 0),
        "value_rows": scatter_about(arg_keys[2], (SEQ, HEADS * E), 1.0, 6.0, ((0, 32), (1, 16)), jnp.float32),
        "teacher_out": scatter_about(arg_keys[3], (SEQ, HEADS * E), 1.0, 6.0, ((0, 512),), jnp.float32),
        "query_map": draw_query_map(jax.random.fold_in(arg_keys[7], 71), 0),
        "key_map": draw_key_map(jax.random.fold_in(arg_keys[7], 71), 0),
        "block_map": draw_block_map(jax.random.fold_in(arg_keys[7], 71), 0),
    }


exact_prec = lax.Precision.HIGHEST


def back_pair(first_half, second_half, grad_feat, half_feat):
    grad_first = grad_feat[..., :half_feat]
    grad_second = grad_feat[..., half_feat:]
    lead = first_half * (grad_first - jnp.sum(first_half * grad_first, axis=-1, keepdims=True))
    trail = second_half * (grad_second - jnp.sum(second_half * grad_second, axis=-1, keepdims=True))
    return lead - trail


def head_grads(queries, keys_in, values_in, target, map_q, map_k):
    pre_q = jnp.dot(queries, map_q, precision=exact_prec, preferred_element_type=jnp.float32)
    pre_k = jnp.dot(keys_in, map_k, precision=exact_prec, preferred_element_type=jnp.float32)
    first_q = jax.nn.softmax(pre_q, axis=-1)
    second_q = jax.nn.softmax(-pre_q, axis=-1)
    first_k = jax.nn.softmax(pre_k, axis=-1)
    second_k = jax.nn.softmax(-pre_k, axis=-1)
    feat_q = jnp.concatenate([first_q, second_q], axis=-1)
    feat_k = jnp.concatenate([first_k, second_k], axis=-1)
    blocks = SEQ // TOK_DEV
    features = 2 * FH
    q_blocks = feat_q.reshape(blocks, TOK_DEV, features)
    k_blocks = feat_k.reshape(blocks, TOK_DEV, features)
    v_blocks = values_in.reshape(blocks, TOK_DEV, E)
    t_blocks = target.reshape(blocks, TOK_DEV, E)
    ladder = jnp.arange(TOK_DEV, dtype=jnp.int32)
    causal = (ladder[:, None] >= ladder[None, :]).astype(jnp.float32)
    zero_pair = (jnp.zeros((features, E), jnp.float32), jnp.zeros((features,), jnp.float32))

    def forward(state_pair, inputs):
        prev_state, prev_norm = state_pair
        blk_q, blk_k, values_b, target_b = inputs
        scores = jnp.dot(blk_q, blk_k.T, precision=exact_prec, preferred_element_type=jnp.float32) * causal
        numerator = jnp.dot(scores, values_b, precision=exact_prec, preferred_element_type=jnp.float32)
        numerator = numerator + jnp.dot(blk_q, prev_state, precision=exact_prec, preferred_element_type=jnp.float32)
        raw_sum = jnp.sum(scores, axis=1) + jnp.dot(blk_q, prev_norm, precision=exact_prec, preferred_element_type=jnp.float32)
        divisor = jnp.maximum(raw_sum, 1.0)
        student = numerator / divisor[:, None]
        mismatch = student - target_b
        grad_num = mismatch / divisor[:, None]
        grad_div = jnp.where(raw_sum > 1.0, -jnp.sum(mismatch * student, axis=1) / divisor, 0.0)
        new_state = prev_state + jnp.dot(blk_k.T, values_b, precision=exact_prec, preferred_element_type=jnp.float32)
        new_norm = prev_norm + jnp.sum(blk_k, axis=0)
        return (new_state, new_norm), (prev_state, prev_norm, grad_num, grad_div)

    unused_pair, saved = lax.scan(forward, zero_pair, (q_blocks, k_blocks, v_blocks, t_blocks))
    prev_states, prev_norms, grad_nums, grad_divs = saved

    def backward(state_pair, inputs):
        next_state, next_norm = state_pair
        blk_q, blk_k, values_b, prev_state, prev_norm, grad_num, grad_div = inputs
        weights = (jnp.dot(grad_num, values_b.T, precision=exact_prec, preferred_element_type=jnp.float32) + grad_div[:, None]) * causal
        grad_fq = jnp.dot(weights, blk_k, precision=exact_prec, preferred_element_type=jnp.float32)
        grad_fq = grad_fq + jnp.dot(grad_num, prev_state.T, precision=exact_prec, preferred_element_type=jnp.float32)
        grad_fq = grad_fq + grad_div[:, None] * prev_norm[None, :]
        grad_fk = jnp.dot(weights.T, blk_q, precision=exact_prec, preferred_element_type=jnp.float32)
        grad_fk = grad_fk + jnp.dot(values_b, next_state.T, precision=exact_prec, preferred_element_type=jnp.float32)
        grad_fk = grad_fk + next_norm[None, :]
        new_state = next_state + jnp.dot(blk_q.T, grad_num, precision=exact_prec, preferred_element_type=jnp.float32)
        new_norm = next_norm + jnp.dot(grad_div, blk_q, precision=exact_prec, preferred_element_type=jnp.float32)
        return (new_state, new_norm), (grad_fq, grad_fk)

    unused_back, grads_blocks = lax.scan(backward, zero_pair, (q_blocks, k_blocks, v_blocks, prev_states, prev_norms, grad_nums, grad_divs), reverse=True)
    grad_fq = grads_blocks[0].reshape(SEQ, features)
    grad_fk = grads_blocks[1].reshape(SEQ, features)
    grad_pq = back_pair(first_q, second_q, grad_fq, FH)
    grad_pk = back_pair(first_k, second_k, grad_fk, FH)
    result_q = jnp.dot(queries.T, grad_pq, precision=exact_prec, preferred_element_type=jnp.float32)
    result_k = jnp.dot(keys_in.T, grad_pk, precision=exact_prec, preferred_element_type=jnp.float32)
    return result_q, result_k


def reference(query_rows, key_rows, value_rows, teacher_out, query_map, key_map, block_map):
    storage_order = jnp.argsort(block_map.reshape(-1)).astype(jnp.int32)
    stored_blocks = teacher_out.reshape(OWNERS * OWNERS, BLK, HEADS * E)
    teacher_seq = jnp.take(stored_blocks, storage_order, axis=0).reshape(SEQ, HEADS * E)
    query_heads = query_rows.reshape(SEQ, HEADS, E).transpose(1, 0, 2)
    key_heads = key_rows.reshape(SEQ, HEADS, E).transpose(1, 0, 2)
    value_heads = value_rows.reshape(SEQ, HEADS, E).transpose(1, 0, 2)
    target_heads = teacher_seq.reshape(SEQ, HEADS, E).transpose(1, 0, 2)

    def one_head(bundle):
        return head_grads(bundle[0], bundle[1], bundle[2], bundle[3], bundle[4], bundle[5])

    head_results = lax.map(one_head, (query_heads, key_heads, value_heads, target_heads, query_map, key_map))
    return head_results[0], head_results[1]
```

```python
import jax
import jax.numpy as jnp
from jax import lax
from jax.sharding import PartitionSpec as P

exact_prec = lax.Precision.HIGHEST
work_prec = lax.Precision.HIGH


def dot(spec, a, b, precision=work_prec):
    return jnp.einsum(spec, a, b, precision=precision, preferred_element_type=jnp.float32)


def exchange(value, axis):
    return lax.all_to_all(value, axis, split_axis=0, concat_axis=0, tiled=True)


def ladder_mask(count, backward):
    rows = lax.broadcasted_iota(jnp.int32, (count, count), 0)
    cols = lax.broadcasted_iota(jnp.int32, (count, count), 1)
    keep = cols > rows if backward else cols < rows
    return keep.astype(jnp.float32)


def scan_state(state, backward):
    count = lax.axis_size("seq")
    features, width = state.shape
    pieces = exchange(state.reshape(count, features // count, width), "seq")
    flat = pieces.reshape(count, features // count * width)
    scanned = dot("is,sc->ic", ladder_mask(count, backward), flat, exact_prec)
    back = exchange(scanned.reshape(pieces.shape), "seq")
    return back.reshape(features, width)


def scan_norm(norm, backward):
    count = lax.axis_size("seq")
    mine = lax.axis_index("seq")
    features = norm.shape[0]
    every = jnp.broadcast_to(norm.reshape(1, features // 128, 128), (count, features // 128, 128))
    every = exchange(every, "seq")
    place = lax.broadcasted_iota(jnp.int32, (count, 1, 1), 0)
    keep = place > mine if backward else place < mine
    return jnp.sum(jnp.where(keep, every, 0.0), axis=0).reshape(features)


def back_pair(first_half, second_half, grad_feat, half_feat):
    grad_first = grad_feat[..., :half_feat]
    grad_second = grad_feat[..., half_feat:]
    lead = first_half * (grad_first - jnp.sum(first_half * grad_first, axis=-1, keepdims=True))
    trail = second_half * (grad_second - jnp.sum(second_half * grad_second, axis=-1, keepdims=True))
    return lead - trail


def relay_teacher(teacher_out, block_map):
    gathered = lax.all_to_all(teacher_out, "head", split_axis=1, concat_axis=0, tiled=True)
    seq_count = lax.axis_size("seq")
    position = lax.axis_index("seq")
    columns = gathered.shape[1]
    block_rows = gathered.shape[0] // seq_count
    blocks = gathered.reshape(seq_count, block_rows, columns)
    slot_ids = lax.dynamic_index_in_dim(block_map, position, 0, keepdims=False)
    owner_ids = slot_ids // seq_count
    ladder = jnp.arange(seq_count, dtype=jnp.int32)
    to_owner = (owner_ids[None, :] == ladder[:, None]).astype(jnp.float32)
    by_owner = jnp.einsum("oj,jrc->orc", to_owner, blocks, precision=exact_prec)
    arrived = exchange(by_owner, "seq")
    own_mask = block_map // seq_count == position
    within = jnp.sum(jnp.where(own_mask, block_map % seq_count, 0), axis=1)
    placing = (within[None, :] == ladder[:, None]).astype(jnp.float32)
    placed = jnp.einsum("is,src->irc", placing, arrived, precision=exact_prec)
    return placed.reshape(seq_count * block_rows, columns)


def sum_slices(term):
    count = lax.axis_size("seq")
    rows, width = term.shape
    return jnp.sum(exchange(term.reshape(count, rows // count, width), "seq"), axis=0)


def per_device(queries, keys, values, teacher_out, query_map, key_map, block_map):
    tokens = queries.shape[0]
    half_feat = query_map.shape[2]
    teacher = relay_teacher(teacher_out, block_map)
    pre_k = dot("te,ef->tf", keys, key_map[0], exact_prec)
    first_k = jax.nn.softmax(pre_k, axis=-1)
    second_k = jax.nn.softmax(-pre_k, axis=-1)
    feat_k = jnp.concatenate([first_k, second_k], axis=-1)
    own_state = dot("tf,te->fe", feat_k, values)
    own_norm = jnp.sum(feat_k, axis=0)
    prev_norm = scan_norm(own_norm, False)
    prev_state = scan_state(own_state, False)
    pre_q = dot("te,ef->tf", queries, query_map[0], exact_prec)
    first_q = jax.nn.softmax(pre_q, axis=-1)
    second_q = jax.nn.softmax(-pre_q, axis=-1)
    feat_q = jnp.concatenate([first_q, second_q], axis=-1)
    ladder = jnp.arange(tokens, dtype=jnp.int32)
    causal = ladder[:, None] >= ladder[None, :]
    scores = jnp.where(causal, dot("tf,sf->ts", feat_q, feat_k), 0.0)
    numerator = dot("ts,se->te", scores, values)
    raw_sum = jnp.sum(scores, axis=-1) + jnp.sum(feat_q * prev_norm[None, :], axis=-1)
    numerator = numerator + dot("tf,fe->te", feat_q, prev_state)
    divisor = jnp.maximum(raw_sum, 1.0)
    student = numerator / divisor[:, None]
    mismatch = student - teacher
    grad_num = mismatch / divisor[:, None]
    grad_div = jnp.where(raw_sum > 1.0, -jnp.sum(mismatch * student, axis=-1) / divisor, 0.0)
    own_back = dot("tf,te->fe", feat_q, grad_num)
    own_back_norm = jnp.sum(grad_div[:, None] * feat_q, axis=0)
    next_norm = scan_norm(own_back_norm, True)
    next_state = scan_state(own_back, True)
    weights = jnp.where(causal, dot("te,se->ts", grad_num, values) + grad_div[:, None], 0.0)
    grad_fq = dot("ts,sf->tf", weights, feat_k)
    grad_fq = grad_fq + dot("te,fe->tf", grad_num, prev_state)
    grad_fq = grad_fq + grad_div[:, None] * prev_norm[None, :]
    grad_pq = back_pair(first_q, second_q, grad_fq, half_feat)
    grad_query = sum_slices(dot("te,tf->ef", queries, grad_pq))
    grad_fk = dot("ts,tf->sf", weights, feat_q)
    grad_fk = grad_fk + dot("se,fe->sf", values, next_state)
    grad_fk = grad_fk + next_norm[None, :]
    grad_pk = back_pair(first_k, second_k, grad_fk, half_feat)
    grad_key = sum_slices(dot("te,tf->ef", keys, grad_pk))
    return (grad_query[None], grad_key[None])


def solution(mesh):
    placed = (
        P("seq", "head"),
        P("seq", "head"),
        P("seq", "head"),
        P(("seq", "head"), None),
        P("head", None, None),
        P("head", None, None),
        P(),
    )
    return jax.shard_map(
        per_device,
        mesh=mesh,
        in_specs=placed,
        out_specs=(P("head", "seq", None), P("head", "seq", None)),
        check_vma=False,
    )
```

```python
import functools

import jax
import jax.numpy as jnp
from jax import lax
from jax.experimental import pallas as pl
from jax.experimental.pallas import tpu as pltpu
from jax.sharding import PartitionSpec as P

exact_prec = lax.Precision.HIGHEST
LANES = 128
CORES = 2
HEAD_WIDTH = 256
ROWS = 8
NN = (((1,), (0,)), ((), ()))
NT = (((1,), (1,)), ((), ()))
TN = (((0,), (0,)), ((), ()))


def halves(x):
    high = x.astype(jnp.bfloat16)
    return high, (x - high.astype(jnp.float32)).astype(jnp.bfloat16)


def dot3(a, b, dims):
    def one(x, y):
        return lax.dot_general(x, y, dims, preferred_element_type=jnp.float32)

    return one(a[0], b[0]) + (one(a[0], b[1]) + one(a[1], b[0]))


def features(rows, weights):
    pre = lax.dot_general(rows, weights, NN, precision=exact_prec, preferred_element_type=jnp.float32)
    first = jnp.exp(pre - jnp.max(pre, axis=-1, keepdims=True))
    second = jnp.exp(jnp.min(pre, axis=-1, keepdims=True) - pre)
    first = first / jnp.sum(first, axis=-1, keepdims=True)
    second = second / jnp.sum(second, axis=-1, keepdims=True)
    return first, second


def pack(out_ref, base, value):
    owners = out_ref.shape[0]
    for c in range(value.shape[1] // LANES):
        part = value[:, c * LANES : (c + 1) * LANES]
        out_ref[:, base + c * ROWS : base + (c + 1) * ROWS, :] = part.reshape(owners, ROWS, LANES)


def unpack(ref, base, count):
    owners = ref.shape[0]
    parts = [
        ref[:, base + c * ROWS : base + (c + 1) * ROWS, :].reshape(owners * ROWS, LANES)
        for c in range(count)
    ]
    return jnp.concatenate(parts, axis=-1)


def pack_norm(out_ref, base, norm):
    owners = out_ref.shape[0]
    count = norm.shape[1] // LANES
    rows = [norm[:, c * LANES : (c + 1) * LANES] for c in range(count)]
    rows.append(jnp.zeros((ROWS - count, LANES), jnp.float32))
    tile = jnp.concatenate(rows, axis=0)
    out_ref[:, base : base + ROWS, :] = jnp.broadcast_to(tile[None], (owners, ROWS, LANES))


def key_kernel(keys, weights, values, feat_ref, out_ref):
    half = weights.shape[1]
    first, second = features(keys[...], weights[...])
    feat_ref[:, :half] = first
    feat_ref[:, half:] = second
    feat = feat_ref[...]
    state = dot3(halves(values[...]), halves(feat), TN)
    width = state.shape[1] // LANES
    pack(out_ref, 0, state)
    pack_norm(out_ref, width * ROWS, jnp.sum(feat, axis=0, keepdims=True))


def query_kernel(queries, weights, feat_k, values, feat_ref, numer_ref, raw_ref):
    half = weights.shape[1]
    tokens = queries.shape[0]
    step = 256
    first, second = features(queries[...], weights[...])
    feat_ref[:, :half] = first
    feat_ref[:, half:] = second
    vals = halves(values[...])
    keys = halves(feat_k[...])
    for lo in range(0, tokens, step):
        hi = lo + step
        fq = halves(feat_ref[lo:hi, :])
        scores = dot3(fq, (keys[0][:hi], keys[1][:hi]), NT)
        t = lax.broadcasted_iota(jnp.int32, scores.shape, 0) + lo
        s = lax.broadcasted_iota(jnp.int32, scores.shape, 1)
        scores = jnp.where(t >= s, scores, 0.0)
        raw_ref[lo:hi, :] = jnp.sum(scores, axis=-1, keepdims=True)
        numer_ref[lo:hi, :] = dot3(halves(scores), (vals[0][:hi], vals[1][:hi]), NN)


def scan_kernel(backward, state_rows, mine_ref, got_ref, out_ref, norm_ref):
    count = got_ref.shape[0]
    mine = mine_ref[0]
    total = jnp.zeros((state_rows, LANES), jnp.float32)
    norm = jnp.zeros((ROWS, LANES), jnp.float32)
    for place in range(count - 1, -1, -1) if backward else range(count):
        out_ref[place, :state_rows, :] = total
        total = total + got_ref[place, :state_rows, :]
        use = (place > mine) if backward else (place < mine)
        tile = got_ref[place, state_rows : state_rows + ROWS, :]
        norm = norm + jnp.where(use, tile, 0.0)
    norm_ref[...] = norm


def partner_kernel(place_ref, teacher_ref, out_ref):
    other = 1 - place_ref[1] % CORES
    width = teacher_ref.shape[1] // place_count(teacher_ref)
    for pair in range(place_count(teacher_ref) // CORES):
        at = pl.multiple_of((pair * CORES + other) * width, width)
        out_ref[:, pair * width : (pair + 1) * width] = teacher_ref[:, pl.ds(at, width)]


def place_count(teacher_ref):
    return teacher_ref.shape[1] // HEAD_WIDTH


def spread_kernel(place_ref, teacher_ref, got_ref, *out_refs):
    core = place_ref[1] % CORES
    chip = place_ref[1] // CORES
    rows = teacher_ref.shape[0]
    ring = len(out_refs)
    mine = pl.multiple_of(core * rows, rows)
    theirs = pl.multiple_of((1 - core) * rows, rows)
    for k, out_ref in enumerate(out_refs):
        to = (chip + k) % ring
        at = pl.multiple_of((to * CORES + core) * HEAD_WIDTH, HEAD_WIDTH)
        out_ref[pl.ds(mine, rows), :] = teacher_ref[:, pl.ds(at, HEAD_WIDTH)]
        at = pl.multiple_of(to * HEAD_WIDTH, HEAD_WIDTH)
        out_ref[pl.ds(theirs, rows), :] = got_ref[:, pl.ds(at, HEAD_WIDTH)]


def forward_scan_kernel(state_rows, rows, place_ref, owner_ref, got_ref, *refs):
    blocks_refs, (out_ref, norm_ref) = refs[:-2], refs[-2:]
    scan_kernel(False, state_rows, place_ref, got_ref, out_ref, norm_ref)
    ring = len(blocks_refs)
    chip = place_ref[1] // CORES
    for k, blocks_ref in enumerate(blocks_refs):
        source = (chip + ring - k) % ring
        each = blocks_ref.shape[0] // rows
        for m in range(each):
            owner = owner_ref[source * each + m]
            for c in range(HEAD_WIDTH // LANES):
                base = state_rows + c * rows
                out_ref[owner, base : base + rows, :] = blocks_ref[
                    m * rows : (m + 1) * rows, c * LANES : (c + 1) * LANES
                ]


def backward_scan_kernel(state_rows, mine_ref, got_ref, term_ref, out_ref, norm_ref):
    scan_kernel(True, state_rows, mine_ref, got_ref, out_ref, norm_ref)
    out_ref[:, state_rows:, :] = term_ref[...]


def norm_row(norm_ref, count):
    return jnp.concatenate([norm_ref[c : c + 1, :] for c in range(count)], axis=-1)


def middle_kernel(
    block_rows, within_ref, got_ref, norm_ref, feat_q, numer, raw,
    state_ref, grad_ref, div_ref, out_ref, teacher_ref,
):
    feats = feat_q.shape[1]
    width = numer.shape[1]
    count = got_ref.shape[0]
    chunks = feats // LANES
    state_rows = chunks * ROWS
    state = unpack(got_ref, 0, chunks)
    state_ref[...] = state
    for source in range(count):
        at = pl.multiple_of(within_ref[source] * block_rows, block_rows)
        for c in range(width // LANES):
            base = state_rows + c * block_rows
            teacher_ref[pl.ds(at, block_rows), c * LANES : (c + 1) * LANES] = got_ref[
                source, base : base + block_rows, :
            ]
    fq = feat_q[...]
    fq_pair = halves(fq)
    numerator = numer[...] + dot3(fq_pair, halves(state), NT)
    prev_norm = norm_row(norm_ref, chunks)
    raw_sum = raw[...] + jnp.sum(fq * prev_norm, axis=-1, keepdims=True)
    divisor = jnp.maximum(raw_sum, 1.0)
    student = numerator / divisor
    mismatch = student - teacher_ref[...]
    grad_num = mismatch / divisor
    grad_div = jnp.where(raw_sum > 1.0, -jnp.sum(mismatch * student, axis=-1, keepdims=True) / divisor, 0.0)
    grad_ref[...] = grad_num
    div_ref[...] = grad_div
    pack(out_ref, 0, dot3(halves(grad_num), fq_pair, TN))
    pack_norm(out_ref, state_rows, jnp.sum(grad_div * fq, axis=0, keepdims=True))


def back_pair(feat, grad, half):
    first, second = feat[:, :half], feat[:, half:]
    grad_first, grad_second = grad[:, :half], grad[:, half:]
    lead = first * (grad_first - jnp.sum(first * grad_first, axis=-1, keepdims=True))
    trail = second * (grad_second - jnp.sum(second * grad_second, axis=-1, keepdims=True))
    return lead - trail


def weight_kernel(
    queries, values, feat_q, feat_k, state, norm_ref, grad_num, grad_div, term_ref, inner_ref, pre_ref
):
    tokens, feats = feat_q.shape
    half = feats // 2
    step = 256
    chunks = feats // LANES
    vals = halves(values[...])
    keys = halves(feat_k[...])
    states = halves(state[...])
    prev_norm = norm_row(norm_ref, chunks)
    for lo in range(0, tokens, step):
        hi = lo + step
        div = grad_div[lo:hi, :]
        num = halves(grad_num[lo:hi, :])
        fq = feat_q[lo:hi, :]
        weights = dot3(num, (vals[0][:hi], vals[1][:hi]), NT) + div
        t = lax.broadcasted_iota(jnp.int32, weights.shape, 0) + lo
        s = lax.broadcasted_iota(jnp.int32, weights.shape, 1)
        weights = halves(jnp.where(t >= s, weights, 0.0))
        grad_fq = dot3(weights, (keys[0][:hi], keys[1][:hi]), NN) + dot3(num, states, NN) + div * prev_norm
        pre_ref[lo:hi, :] = back_pair(fq, grad_fq, half)
        part = dot3(weights, halves(fq), TN)
        if lo == 0:
            inner_ref[:hi, :] = part
        else:
            inner_ref[:lo, :] = inner_ref[:lo, :] + part[:lo]
            inner_ref[lo:hi, :] = part[lo:]
    pack(term_ref, 0, dot3(halves(queries[...]), halves(pre_ref[...]), TN))


def close_kernel(keys, values, feat_k, inner, got_ref, norm_ref, term_ref, query_ref):
    feats = feat_k.shape[1]
    chunks = feats // LANES
    state = unpack(got_ref, 0, chunks)
    grad_fk = inner[...] + dot3(halves(values[...]), halves(state), NN) + norm_row(norm_ref, chunks)
    grad_pk = back_pair(feat_k[...], grad_fk, feats // 2)
    pack(term_ref, 0, dot3(halves(keys[...]), halves(grad_pk), TN))
    sum_kernel(chunks * ROWS, got_ref, query_ref)


def sum_kernel(base, got_ref, out_ref):
    for c in range(out_ref.shape[1] // LANES):
        part = got_ref[:, base + c * ROWS : base + (c + 1) * ROWS, :]
        out_ref[:, c * LANES : (c + 1) * LANES] = jnp.sum(part, axis=0)


def call(body, outs, spaces, cost, args, scratch=()):
    vmem = pl.BlockSpec(memory_space=pltpu.VMEM)
    smem = pl.BlockSpec(memory_space=pltpu.SMEM)
    return pl.pallas_call(
        body,
        out_shape=[jax.ShapeDtypeStruct(shape, jnp.float32) for shape in outs],
        in_specs=[smem if kind == "s" else vmem for kind in spaces],
        out_specs=[vmem] * len(outs),
        scratch_shapes=[pltpu.VMEM(shape, jnp.float32) for shape in scratch],
        compiler_params=pltpu.CompilerParams(vmem_limit_bytes=24 * 1024 * 1024),
        cost_estimate=pl.CostEstimate(flops=int(cost * 1e9), bytes_accessed=1 << 20, transcendentals=0),
    )(*args)


def exchange(value, axis):
    return lax.all_to_all(value, axis, split_axis=0, concat_axis=0, tiled=True)


def per_device(queries, keys, values, teacher_out, query_map, key_map, block_map):
    tokens, width = queries.shape
    half = query_map.shape[2]
    feats = 2 * half
    count = lax.axis_size("seq")
    mine = lax.axis_index("seq")
    heads = lax.axis_size("head")
    chunks = feats // LANES
    state_rows = chunks * ROWS
    block_rows = tokens // count
    term_rows = half // LANES * ROWS

    place = jnp.stack([mine, lax.axis_index("head")]).astype(jnp.int32)
    slot_ids = lax.dynamic_index_in_dim(block_map, mine, 0, keepdims=False)
    owner_ids = slot_ids // count
    within = jnp.sum(jnp.where(block_map // count == mine, block_map % count, 0), axis=1).astype(jnp.int32)
    ring = heads // CORES
    rows = teacher_out.shape[0]
    (partner,) = call(partner_kernel, [(rows, ring * width)], "sv", 0.1, (place, teacher_out))
    partner = lax.ppermute(partner, "head", [(h, h ^ 1) for h in range(heads)])
    feat_k, out1 = call(
        key_kernel, [(tokens, feats), (count, state_rows + ROWS, LANES)], "vvv", 1.0,
        (keys, key_map[0], values),
    )
    got1 = exchange(out1, "seq")
    blocks = call(spread_kernel, [(CORES * rows, width)] * ring, "svv", 0.1, (place, teacher_out, partner))
    blocks = list(blocks[:1]) + [
        lax.ppermute(blocks[k], "head", [(h, (h + CORES * k) % heads) for h in range(heads)])
        for k in range(1, ring)
    ]
    feat_q, numer, raw = call(
        query_kernel, [(tokens, feats), (tokens, width), (tokens, 1)], "vvvv", 2.0,
        (queries, query_map[0], feat_k, values),
    )
    out2, prev_norm = call(
        functools.partial(forward_scan_kernel, state_rows, block_rows),
        [(count, state_rows + block_rows * (width // LANES), LANES), (ROWS, LANES)],
        "ssv" + "v" * ring, 0.1, (place, owner_ids, got1, *blocks),
    )
    got2 = exchange(out2, "seq")
    state, grad_num, grad_div, out3 = call(
        functools.partial(middle_kernel, block_rows),
        [(width, feats), (tokens, width), (tokens, 1), (count, state_rows + ROWS, LANES)],
        "svvvvv", 1.0, (within, got2, prev_norm, feat_q, numer, raw), [(tokens, width)],
    )
    got3 = exchange(out3, "seq")
    term_q, inner = call(
        weight_kernel, [(count, term_rows, LANES), (tokens, feats)], "vvvvvvvv", 4.0,
        (queries, values, feat_q, feat_k, state, prev_norm, grad_num, grad_div), [(tokens, half)],
    )
    out4, next_norm = call(
        functools.partial(backward_scan_kernel, state_rows),
        [(count, state_rows + term_rows, LANES), (ROWS, LANES)],
        "svv", 0.1, (place, got3, term_q),
    )
    got4 = exchange(out4, "seq")
    out5, grad_query = call(
        close_kernel, [(count, term_rows, LANES), (width // count, half)], "vvvvvv", 1.0,
        (keys, values, feat_k, inner, got4, next_norm),
    )
    got5 = exchange(out5, "seq")
    (grad_key,) = call(functools.partial(sum_kernel, 0), [(width // count, half)], "v", 0.1, (got5,))
    return (grad_query[None], grad_key[None])


def solution(mesh):
    placed = (
        P("seq", "head"),
        P("seq", "head"),
        P("seq", "head"),
        P(("seq", "head"), None),
        P("head", None, None),
        P("head", None, None),
        P(),
    )
    return jax.shard_map(
        per_device,
        mesh=mesh,
        in_specs=placed,
        out_specs=(P("head", "seq", None), P("head", "seq", None)),
        check_vma=False,
    )
```

```python
import functools

import jax
import jax.numpy as jnp
from jax import lax
from jax.experimental import pallas as pl
from jax.experimental.pallas import tpu as pltpu
from jax.sharding import PartitionSpec as P

exact_prec = lax.Precision.HIGHEST
LANES = 128
ROWS = 8
NN = (((1,), (0,)), ((), ()))
NT = (((1,), (1,)), ((), ()))
TN = (((0,), (0,)), ((), ()))


def halves(x):
    high = x.astype(jnp.bfloat16)
    return high, (x - high.astype(jnp.float32)).astype(jnp.bfloat16)


def dot3(a, b, dims):
    def one(x, y):
        return lax.dot_general(x, y, dims, preferred_element_type=jnp.float32)

    return one(a[0], b[0]) + (one(a[0], b[1]) + one(a[1], b[0]))


def features(rows, weights):
    pre = lax.dot_general(rows, weights, NN, precision=exact_prec, preferred_element_type=jnp.float32)
    first = jnp.exp(pre - jnp.max(pre, axis=-1, keepdims=True))
    second = jnp.exp(jnp.min(pre, axis=-1, keepdims=True) - pre)
    first = first / jnp.sum(first, axis=-1, keepdims=True)
    second = second / jnp.sum(second, axis=-1, keepdims=True)
    return first, second


def pack(out_ref, base, value):
    owners = out_ref.shape[0]
    for c in range(value.shape[1] // LANES):
        part = value[:, c * LANES : (c + 1) * LANES]
        out_ref[:, base + c * ROWS : base + (c + 1) * ROWS, :] = part.reshape(owners, ROWS, LANES)


def unpack(ref, base, count):
    owners = ref.shape[0]
    parts = [
        ref[:, base + c * ROWS : base + (c + 1) * ROWS, :].reshape(owners * ROWS, LANES)
        for c in range(count)
    ]
    return jnp.concatenate(parts, axis=-1)


def pack_norm(out_ref, base, norm):
    owners = out_ref.shape[0]
    count = norm.shape[1] // LANES
    rows = [norm[:, c * LANES : (c + 1) * LANES] for c in range(count)]
    rows.append(jnp.zeros((ROWS - count, LANES), jnp.float32))
    tile = jnp.concatenate(rows, axis=0)
    out_ref[:, base : base + ROWS, :] = jnp.broadcast_to(tile[None], (owners, ROWS, LANES))


def key_kernel(keys, weights, values, feat_ref, out_ref):
    half = weights.shape[1]
    first, second = features(keys[...], weights[...])
    feat_ref[:, :half] = first
    feat_ref[:, half:] = second
    feat = feat_ref[...]
    state = dot3(halves(values[...]), halves(feat), TN)
    width = state.shape[1] // LANES
    pack(out_ref, 0, state)
    pack_norm(out_ref, width * ROWS, jnp.sum(feat, axis=0, keepdims=True))


def query_kernel(queries, weights, feat_k, values, out_ref):
    half = weights.shape[1]
    tokens, width = queries.shape
    feats = 2 * half
    step = 256
    first, second = features(queries[...], weights[...])
    out_ref[:, :half] = first
    out_ref[:, half:feats] = second
    vals = halves(values[...])
    keys = halves(feat_k[...])
    for lo in range(0, tokens, step):
        hi = lo + step
        fq = halves(out_ref[lo:hi, :feats])
        scores = dot3(fq, (keys[0][:hi], keys[1][:hi]), NT)
        t = lax.broadcasted_iota(jnp.int32, scores.shape, 0) + lo
        s = lax.broadcasted_iota(jnp.int32, scores.shape, 1)
        scores = jnp.where(t >= s, scores, 0.0)
        raw = jnp.sum(scores, axis=-1, keepdims=True)
        out_ref[lo:hi, feats + width :] = jnp.broadcast_to(raw, (step, LANES))
        out_ref[lo:hi, feats : feats + width] = dot3(halves(scores), (vals[0][:hi], vals[1][:hi]), NN)


def scan_kernel(backward, state_rows, mine_ref, got_ref, out_ref, norm_ref):
    count = got_ref.shape[0]
    mine = mine_ref[0]
    total = jnp.zeros((state_rows, LANES), jnp.float32)
    norm = jnp.zeros((ROWS, LANES), jnp.float32)
    for place in range(count - 1, -1, -1) if backward else range(count):
        out_ref[place, :state_rows, :] = total
        total = total + got_ref[place, :state_rows, :]
        use = (place > mine) if backward else (place < mine)
        tile = got_ref[place, state_rows : state_rows + ROWS, :]
        norm = norm + jnp.where(use, tile, 0.0)
    norm_ref[...] = norm


def forward_scan_kernel(state_rows, mine_ref, owner_ref, got_ref, blocks_ref, out_ref, norm_ref):
    scan_kernel(False, state_rows, mine_ref, got_ref, out_ref, norm_ref)
    count, rows, width = blocks_ref.shape
    for place in range(count):
        owner = owner_ref[place]
        for c in range(width // LANES):
            base = state_rows + c * rows
            out_ref[owner, base : base + rows, :] = blocks_ref[place, :, c * LANES : (c + 1) * LANES]


def backward_scan_kernel(state_rows, mine_ref, got_ref, term_ref, out_ref, norm_ref):
    scan_kernel(True, state_rows, mine_ref, got_ref, out_ref, norm_ref)
    out_ref[:, state_rows:, :] = term_ref[...]


def norm_row(norm_ref, count):
    return jnp.concatenate([norm_ref[c : c + 1, :] for c in range(count)], axis=-1)


def middle_kernel(
    block_rows, feats, within_ref, got_ref, norm_ref, block_ref, grad_ref, out_ref, teacher_ref
):
    width = teacher_ref.shape[1]
    count = got_ref.shape[0]
    chunks = feats // LANES
    state_rows = chunks * ROWS
    state = unpack(got_ref, 0, chunks)
    for source in range(count):
        at = pl.multiple_of(within_ref[source] * block_rows, block_rows)
        for c in range(width // LANES):
            base = state_rows + c * block_rows
            teacher_ref[pl.ds(at, block_rows), c * LANES : (c + 1) * LANES] = got_ref[
                source, base : base + block_rows, :
            ]
    fq = block_ref[:, :feats]
    fq_pair = halves(fq)
    numerator = block_ref[:, feats : feats + width] + dot3(fq_pair, halves(state), NT)
    prev_norm = norm_row(norm_ref, chunks)
    raw_sum = block_ref[:, feats + width : feats + width + 1] + jnp.sum(fq * prev_norm, axis=-1, keepdims=True)
    divisor = jnp.maximum(raw_sum, 1.0)
    student = numerator / divisor
    mismatch = student - teacher_ref[...]
    grad_num = mismatch / divisor
    grad_div = jnp.where(raw_sum > 1.0, -jnp.sum(mismatch * student, axis=-1, keepdims=True) / divisor, 0.0)
    grad_ref[:, :width] = grad_num
    grad_ref[:, width:] = jnp.broadcast_to(grad_div, (grad_div.shape[0], LANES))
    pack(out_ref, 0, dot3(halves(grad_num), fq_pair, TN))
    pack_norm(out_ref, state_rows, jnp.sum(grad_div * fq, axis=0, keepdims=True))


def back_pair(feat, grad, half):
    first, second = feat[:, :half], feat[:, half:]
    grad_first, grad_second = grad[:, :half], grad[:, half:]
    lead = first * (grad_first - jnp.sum(first * grad_first, axis=-1, keepdims=True))
    trail = second * (grad_second - jnp.sum(second * grad_second, axis=-1, keepdims=True))
    return lead - trail


def weight_kernel(
    queries, values, block_ref, feat_k, got_ref, norm_ref, grad_ref, term_ref, inner_ref, pre_ref
):
    tokens, feats = feat_k.shape
    width = values.shape[1]
    half = feats // 2
    step = 256
    chunks = feats // LANES
    vals = halves(values[...])
    keys = halves(feat_k[...])
    states = halves(unpack(got_ref, 0, chunks))
    prev_norm = norm_row(norm_ref, chunks)
    for lo in range(0, tokens, step):
        hi = lo + step
        div = grad_ref[lo:hi, width : width + 1]
        num = halves(grad_ref[lo:hi, :width])
        fq = block_ref[lo:hi, :feats]
        weights = dot3(num, (vals[0][:hi], vals[1][:hi]), NT) + div
        t = lax.broadcasted_iota(jnp.int32, weights.shape, 0) + lo
        s = lax.broadcasted_iota(jnp.int32, weights.shape, 1)
        weights = halves(jnp.where(t >= s, weights, 0.0))
        grad_fq = dot3(weights, (keys[0][:hi], keys[1][:hi]), NN) + dot3(num, states, NN) + div * prev_norm
        pre_ref[lo:hi, :] = back_pair(fq, grad_fq, half)
        part = dot3(weights, halves(fq), TN)
        if lo == 0:
            inner_ref[:hi, :] = part
        else:
            inner_ref[:lo, :] = inner_ref[:lo, :] + part[:lo]
            inner_ref[lo:hi, :] = part[lo:]
    pack(term_ref, 0, dot3(halves(queries[...]), halves(pre_ref[...]), TN))


def close_kernel(keys, values, feat_k, inner, got_ref, norm_ref, term_ref, query_ref):
    feats = feat_k.shape[1]
    chunks = feats // LANES
    state = unpack(got_ref, 0, chunks)
    grad_fk = inner[...] + dot3(halves(values[...]), halves(state), NN) + norm_row(norm_ref, chunks)
    grad_pk = back_pair(feat_k[...], grad_fk, feats // 2)
    pack(term_ref, 0, dot3(halves(keys[...]), halves(grad_pk), TN))
    sum_kernel(chunks * ROWS, got_ref, query_ref)


def sum_kernel(base, got_ref, out_ref):
    for c in range(out_ref.shape[1] // LANES):
        part = got_ref[:, base + c * ROWS : base + (c + 1) * ROWS, :]
        out_ref[:, c * LANES : (c + 1) * LANES] = jnp.sum(part, axis=0)


def call(body, outs, spaces, cost, args, scratch=()):
    vmem = pl.BlockSpec(memory_space=pltpu.VMEM)
    smem = pl.BlockSpec(memory_space=pltpu.SMEM)
    return pl.pallas_call(
        body,
        out_shape=[jax.ShapeDtypeStruct(shape, jnp.float32) for shape in outs],
        in_specs=[smem if kind == "s" else vmem for kind in spaces],
        out_specs=[vmem] * len(outs),
        scratch_shapes=[pltpu.VMEM(shape, jnp.float32) for shape in scratch],
        compiler_params=pltpu.CompilerParams(vmem_limit_bytes=24 * 1024 * 1024),
        cost_estimate=pl.CostEstimate(flops=int(cost * 1e9), bytes_accessed=1 << 20, transcendentals=0),
    )(*args)


def exchange(value, axis):
    return lax.all_to_all(value, axis, split_axis=0, concat_axis=0, tiled=True)


def per_device(queries, keys, values, teacher_out, query_map, key_map, block_map):
    tokens, width = queries.shape
    half = query_map.shape[2]
    feats = 2 * half
    count = lax.axis_size("seq")
    mine = lax.axis_index("seq")
    chunks = feats // LANES
    state_rows = chunks * ROWS
    block_rows = tokens // count
    term_rows = half // LANES * ROWS

    place = mine.astype(jnp.int32).reshape(1)
    slot_ids = lax.dynamic_index_in_dim(block_map, mine, 0, keepdims=False)
    owner_ids = slot_ids // count
    within = jnp.sum(jnp.where(block_map // count == mine, block_map % count, 0), axis=1).astype(jnp.int32)
    gathered = lax.all_to_all(teacher_out, "head", split_axis=1, concat_axis=0, tiled=True)
    blocks = gathered.reshape(count, block_rows, width)

    feat_k, out1 = call(
        key_kernel, [(tokens, feats), (count, state_rows + ROWS, LANES)], "vvv", 1.0,
        (keys, key_map[0], values),
    )
    got1 = exchange(out1, "seq")
    (block,) = call(
        query_kernel, [(tokens, feats + width + LANES)], "vvvv", 2.0,
        (queries, query_map[0], feat_k, values),
    )
    out2, prev_norm = call(
        functools.partial(forward_scan_kernel, state_rows),
        [(count, state_rows + block_rows * (width // LANES), LANES), (ROWS, LANES)],
        "ssvv", 0.1, (place, owner_ids, got1, blocks),
    )
    got2 = exchange(out2, "seq")
    grads, out3 = call(
        functools.partial(middle_kernel, block_rows, feats),
        [(tokens, width + LANES), (count, state_rows + ROWS, LANES)],
        "svvv", 1.0, (within, got2, prev_norm, block), [(tokens, width)],
    )
    got3 = exchange(out3, "seq")
    term_q, inner = call(
        weight_kernel, [(count, term_rows, LANES), (tokens, feats)], "vvvvvvv", 4.0,
        (queries, values, block, feat_k, got2, prev_norm, grads), [(tokens, half)],
    )
    out4, next_norm = call(
        functools.partial(backward_scan_kernel, state_rows),
        [(count, state_rows + term_rows, LANES), (ROWS, LANES)],
        "svv", 0.1, (place, got3, term_q),
    )
    got4 = exchange(out4, "seq")
    out5, grad_query = call(
        close_kernel, [(count, term_rows, LANES), (width // count, half)], "vvvvvv", 1.0,
        (keys, values, feat_k, inner, got4, next_norm),
    )
    got5 = exchange(out5, "seq")
    (grad_key,) = call(functools.partial(sum_kernel, 0), [(width // count, half)], "v", 0.1, (got5,))
    return (grad_query[None], grad_key[None])


def solution(mesh):
    placed = (
        P("seq", "head"),
        P("seq", "head"),
        P("seq", "head"),
        P(("seq", "head"), None),
        P("head", None, None),
        P("head", None, None),
        P(),
    )
    return jax.shard_map(
        per_device,
        mesh=mesh,
        in_specs=placed,
        out_specs=(P("head", "seq", None), P("head", "seq", None)),
        check_vma=False,
    )
```

```python
import functools

import jax
import jax.numpy as jnp
from jax import lax
from jax.experimental import pallas as pl
from jax.experimental.pallas import tpu as pltpu
from jax.sharding import PartitionSpec as P


exact_prec = lax.Precision.HIGHEST
LANES = 128
NORM_ROWS = 4
ROWS = 8
NN = (((1,), (0,)), ((), ()))
NT = (((1,), (1,)), ((), ()))
TN = (((0,), (0,)), ((), ()))


def halves(x):
    high = x.astype(jnp.bfloat16)
    return high, (x - high.astype(jnp.float32)).astype(jnp.bfloat16)


def dot3(a, b, dims):
    def one(x, y):
        return lax.dot_general(x, y, dims, preferred_element_type=jnp.float32)

    return one(a[0], b[0]) + (one(a[0], b[1]) + one(a[1], b[0]))


def features(rows, weights):
    pre = lax.dot_general(rows, weights, NN, precision=exact_prec, preferred_element_type=jnp.float32)
    first = jnp.exp(pre - jnp.max(pre, axis=-1, keepdims=True))
    second = jnp.exp(jnp.min(pre, axis=-1, keepdims=True) - pre)
    first = first / jnp.sum(first, axis=-1, keepdims=True)
    second = second / jnp.sum(second, axis=-1, keepdims=True)
    return first, second


def pack(out_ref, base, value):
    owners = out_ref.shape[0]
    for c in range(value.shape[1] // LANES):
        part = value[:, c * LANES : (c + 1) * LANES]
        out_ref[:, base + c * ROWS : base + (c + 1) * ROWS, :] = part.reshape(owners, ROWS, LANES)


def unpack(ref, base, count):
    owners = ref.shape[0]
    parts = [
        ref[:, base + c * ROWS : base + (c + 1) * ROWS, :].reshape(owners * ROWS, LANES)
        for c in range(count)
    ]
    return jnp.concatenate(parts, axis=-1)


def norm_tile(norm):
    count = norm.shape[1] // LANES
    rows = [norm[:, c * LANES : (c + 1) * LANES] for c in range(count)]
    rows.append(jnp.zeros((ROWS - count, LANES), jnp.float32))
    return jnp.concatenate(rows, axis=0)


def pack_norm(out_ref, base, norm):
    owners = out_ref.shape[0]
    tile = norm_tile(norm)
    out_ref[:, base : base + ROWS, :] = jnp.broadcast_to(tile[None], (owners, ROWS, LANES))


def key_kernel(place_ref, keys, weights, values, feat_ref, send_ref, keep_ref):
    half = weights.shape[1]
    first, second = features(keys[...], weights[...])
    feat_ref[:, :half] = first
    feat_ref[:, half:] = second
    feat = feat_ref[...]
    state = dot3(halves(values[...]), halves(feat), TN)
    split = state.shape[0] // 2
    odd = place_ref[0] % 2 == 1
    low, high = state[:split], state[split:]
    slices = split // ROWS
    norm = norm_tile(jnp.sum(feat, axis=0, keepdims=True))
    for ref, value in ((send_ref, jnp.where(odd, low, high)), (keep_ref, jnp.where(odd, high, low))):
        for c in range(value.shape[1] // LANES):
            part = value[:, c * LANES : (c + 1) * LANES]
            ref[:slices, c * ROWS : (c + 1) * ROWS, :] = part.reshape(slices, ROWS, LANES)
        ref[slices, :ROWS, :] = norm
        ref[slices, ROWS:, :] = jnp.zeros_like(ref[slices, ROWS:, :])


def pair_kernel(place_ref, keep_ref, got_ref, out_ref):
    slices, rows, _ = out_ref.shape
    rows -= ROWS
    odd = place_ref[0] % 2 == 1
    out_ref[:, :rows, :] = keep_ref[:slices] + got_ref[:slices]
    mine, other = keep_ref[slices, :NORM_ROWS, :], got_ref[slices, :NORM_ROWS, :]
    tile = jnp.concatenate([jnp.where(odd, other, mine), jnp.where(odd, mine, other)], axis=0)
    out_ref[:, rows:, :] = jnp.broadcast_to(tile[None], (slices, ROWS, LANES))


def unpack_half(ref):
    slices = ref.shape[0] - 1
    return jnp.concatenate(
        [
            ref[:slices, c * ROWS : (c + 1) * ROWS, :].reshape(slices * ROWS, LANES)
            for c in range(ref.shape[1] // ROWS)
        ],
        axis=-1,
    )


def even_state(place_ref, low_ref, high_ref):
    odd = place_ref[0] % 2 == 1
    both = jnp.concatenate([unpack_half(low_ref), unpack_half(high_ref)], axis=0)
    return jnp.where(odd, both, 0.0)


def unpack_pairs(ref, count):
    pairs = ref.shape[0] // 2
    halves_of = []
    for parity in range(2):
        parts = []
        for c in range(count):
            part = ref[:, c * ROWS : (c + 1) * ROWS, :].reshape(pairs, 2, ROWS, LANES)
            parts.append(part[:, parity].reshape(pairs * ROWS, LANES))
        halves_of.append(jnp.concatenate(parts, axis=-1))
    return jnp.concatenate(halves_of, axis=0)


def query_kernel(place_ref, queries, weights, feat_k, values, low_ref, high_ref, out_ref):
    half = weights.shape[1]
    tokens, width = queries.shape
    feats = 2 * half
    step = 256
    first, second = features(queries[...], weights[...])
    out_ref[:, :half] = first
    out_ref[:, half:feats] = second
    vals = halves(values[...])
    keys = halves(feat_k[...])
    before = halves(even_state(place_ref, low_ref, high_ref))
    for lo in range(0, tokens, step):
        hi = lo + step
        fq = halves(out_ref[lo:hi, :feats])
        scores = dot3(fq, (keys[0][:hi], keys[1][:hi]), NT)
        t = lax.broadcasted_iota(jnp.int32, scores.shape, 0) + lo
        s = lax.broadcasted_iota(jnp.int32, scores.shape, 1)
        scores = jnp.where(t >= s, scores, 0.0)
        raw = jnp.sum(scores, axis=-1, keepdims=True)
        out_ref[lo:hi, feats + width :] = jnp.broadcast_to(raw, (step, LANES))
        numer = dot3(halves(scores), (vals[0][:hi], vals[1][:hi]), NN)
        out_ref[lo:hi, feats : feats + width] = numer + dot3(fq, before, NT)


def forward_scan_kernel(state_rows, place_ref, owner_ref, got_ref, blocks_ref, out_ref, norm_ref):
    pairs = got_ref.shape[0]
    mine = place_ref[0] // 2
    odd = place_ref[0] % 2 == 1
    total = jnp.zeros((state_rows, LANES), jnp.float32)
    norm = jnp.zeros((NORM_ROWS, LANES), jnp.float32)
    for pair in range(pairs):
        out_ref[2 * pair, :state_rows, :] = total
        out_ref[2 * pair + 1, :state_rows, :] = total
        total = total + got_ref[pair, :state_rows, :]
        even = got_ref[pair, state_rows : state_rows + NORM_ROWS, :]
        last = got_ref[pair, state_rows + NORM_ROWS :, :]
        use_even = (pair < mine) | ((pair == mine) & odd)
        norm = norm + jnp.where(use_even, even, 0.0)
        norm = norm + jnp.where(pair < mine, last, 0.0)
    norm_ref[...] = jnp.concatenate([norm, jnp.zeros_like(norm)], axis=0)
    count, rows, width = blocks_ref.shape
    for place in range(count):
        owner = owner_ref[place]
        for c in range(width // LANES):
            base = state_rows + c * rows
            out_ref[owner, base : base + rows, :] = blocks_ref[place, :, c * LANES : (c + 1) * LANES]


def backward_scan_kernel(state_rows, place_ref, got_ref, term_ref, out_ref, norm_ref):
    mine = place_ref[0]
    total = jnp.zeros((state_rows, LANES), jnp.float32)
    norm = jnp.zeros((ROWS, LANES), jnp.float32)
    for place in range(got_ref.shape[0] - 1, -1, -1):
        out_ref[place, :state_rows, :] = total
        total = total + got_ref[place, :state_rows, :]
        norm = norm + jnp.where(place > mine, got_ref[place, state_rows:, :], 0.0)
    norm_ref[...] = norm
    out_ref[:, state_rows:, :] = term_ref[...]


def norm_row(norm_ref, count):
    return jnp.concatenate([norm_ref[c : c + 1, :] for c in range(count)], axis=-1)


def middle_kernel(
    block_rows, feats, within_ref, got_ref, norm_ref, block_ref, grad_ref, out_ref, teacher_ref
):
    width = teacher_ref.shape[1]
    count = got_ref.shape[0]
    chunks = feats // LANES
    state_rows = chunks * ROWS
    state = unpack_pairs(got_ref, chunks)
    for source in range(count):
        at = pl.multiple_of(within_ref[source] * block_rows, block_rows)
        for c in range(width // LANES):
            base = state_rows + c * block_rows
            teacher_ref[pl.ds(at, block_rows), c * LANES : (c + 1) * LANES] = got_ref[
                source, base : base + block_rows, :
            ]
    fq = block_ref[:, :feats]
    fq_pair = halves(fq)
    numerator = block_ref[:, feats : feats + width] + dot3(fq_pair, halves(state), NT)
    prev_norm = norm_row(norm_ref, chunks)
    raw_sum = block_ref[:, feats + width : feats + width + 1] + jnp.sum(fq * prev_norm, axis=-1, keepdims=True)
    divisor = jnp.maximum(raw_sum, 1.0)
    student = numerator / divisor
    mismatch = student - teacher_ref[...]
    grad_num = mismatch / divisor
    grad_div = jnp.where(raw_sum > 1.0, -jnp.sum(mismatch * student, axis=-1, keepdims=True) / divisor, 0.0)
    grad_ref[:, :width] = grad_num
    grad_ref[:, width:] = jnp.broadcast_to(grad_div, (grad_div.shape[0], LANES))
    pack(out_ref, 0, dot3(halves(grad_num), fq_pair, TN))
    pack_norm(out_ref, state_rows, jnp.sum(grad_div * fq, axis=0, keepdims=True))


def back_pair(feat, grad, half):
    first, second = feat[:, :half], feat[:, half:]
    grad_first, grad_second = grad[:, :half], grad[:, half:]
    lead = first * (grad_first - jnp.sum(first * grad_first, axis=-1, keepdims=True))
    trail = second * (grad_second - jnp.sum(second * grad_second, axis=-1, keepdims=True))
    return lead - trail


def weight_kernel(
    place_ref, queries, values, block_ref, feat_k, got_ref, norm_ref, grad_ref, low_ref, high_ref,
    term_ref, inner_ref, pre_ref,
):
    tokens, feats = feat_k.shape
    width = values.shape[1]
    half = feats // 2
    step = 256
    chunks = feats // LANES
    vals = halves(values[...])
    keys = halves(feat_k[...])
    states = halves(unpack_pairs(got_ref, chunks) + even_state(place_ref, low_ref, high_ref))
    prev_norm = norm_row(norm_ref, chunks)
    for lo in range(0, tokens, step):
        hi = lo + step
        div = grad_ref[lo:hi, width : width + 1]
        num = halves(grad_ref[lo:hi, :width])
        fq = block_ref[lo:hi, :feats]
        weights = dot3(num, (vals[0][:hi], vals[1][:hi]), NT) + div
        t = lax.broadcasted_iota(jnp.int32, weights.shape, 0) + lo
        s = lax.broadcasted_iota(jnp.int32, weights.shape, 1)
        weights = halves(jnp.where(t >= s, weights, 0.0))
        grad_fq = dot3(weights, (keys[0][:hi], keys[1][:hi]), NN) + dot3(num, states, NN) + div * prev_norm
        pre_ref[lo:hi, :] = back_pair(fq, grad_fq, half)
        part = dot3(weights, halves(fq), TN)
        if lo == 0:
            inner_ref[:hi, :] = part
        else:
            inner_ref[:lo, :] = inner_ref[:lo, :] + part[:lo]
            inner_ref[lo:hi, :] = part[lo:]
    pack(term_ref, 0, dot3(halves(queries[...]), halves(pre_ref[...]), TN))


def close_kernel(keys, values, feat_k, inner, got_ref, norm_ref, term_ref, query_ref):
    feats = feat_k.shape[1]
    chunks = feats // LANES
    state = unpack(got_ref, 0, chunks)
    grad_fk = inner[...] + dot3(halves(values[...]), halves(state), NN) + norm_row(norm_ref, chunks)
    grad_pk = back_pair(feat_k[...], grad_fk, feats // 2)
    pack(term_ref, 0, dot3(halves(keys[...]), halves(grad_pk), TN))
    sum_kernel(chunks * ROWS, got_ref, query_ref)


def sum_kernel(base, got_ref, out_ref):
    for c in range(out_ref.shape[1] // LANES):
        part = got_ref[:, base + c * ROWS : base + (c + 1) * ROWS, :]
        out_ref[:, c * LANES : (c + 1) * LANES] = jnp.sum(part, axis=0)


def call(body, outs, spaces, cost, args, scratch=()):
    vmem = pl.BlockSpec(memory_space=pltpu.VMEM)
    smem = pl.BlockSpec(memory_space=pltpu.SMEM)
    return pl.pallas_call(
        body,
        out_shape=[jax.ShapeDtypeStruct(shape, jnp.float32) for shape in outs],
        in_specs=[smem if kind == "s" else vmem for kind in spaces],
        out_specs=[vmem] * len(outs),
        scratch_shapes=[pltpu.VMEM(shape, jnp.float32) for shape in scratch],
        compiler_params=pltpu.CompilerParams(vmem_limit_bytes=24 * 1024 * 1024),
        cost_estimate=pl.CostEstimate(flops=int(cost * 1e9), bytes_accessed=1 << 20, transcendentals=0),
    )(*args)


def cut_kernel(in_ref, out_ref, sems):
    heads, _, width = out_ref.shape
    copies = [
        pltpu.make_async_copy(in_ref.at[:, pl.ds(h * width, width)], out_ref.at[h], sems.at[h])
        for h in range(heads)
    ]
    for copy in copies:
        copy.start()
    for copy in copies:
        copy.wait()


def cut_heads(rows, heads):
    count, total = rows.shape
    return pl.pallas_call(
        cut_kernel,
        out_shape=jax.ShapeDtypeStruct((heads, count, total // heads), rows.dtype),
        in_specs=[pl.BlockSpec(memory_space=pl.ANY)],
        out_specs=pl.BlockSpec(memory_space=pltpu.VMEM),
        scratch_shapes=[pltpu.SemaphoreType.DMA((heads,))],
        name="cut",
    )(rows)


def exchange(value, axis):
    return lax.all_to_all(value, axis, split_axis=0, concat_axis=0, tiled=True)


def per_device(queries, keys, values, teacher_out, query_map, key_map, block_map):
    tokens, width = queries.shape
    half = query_map.shape[2]
    feats = 2 * half
    count = lax.axis_size("seq")
    mine = lax.axis_index("seq")
    heads = lax.axis_size("head")
    chunks = feats // LANES
    state_rows = chunks * ROWS
    block_rows = tokens // count
    term_rows = half // LANES * ROWS

    place = mine.astype(jnp.int32).reshape(1)
    slot_ids = lax.dynamic_index_in_dim(block_map, mine, 0, keepdims=False)
    owner_ids = slot_ids // count
    within = jnp.sum(jnp.where(block_map // count == mine, block_map % count, 0), axis=1).astype(jnp.int32)
    gathered = exchange(cut_heads(teacher_out, heads), "head")
    blocks = gathered.reshape(count, block_rows, width)

    slices = count // 2
    half_shape = (slices + 1, state_rows, LANES)
    feat_k, send, keep = call(
        key_kernel, [(tokens, feats), half_shape, half_shape], "svvv", 1.0,
        (place, keys, key_map[0], values),
    )
    swapped = lax.ppermute(send, "seq", [(s, s ^ 1) for s in range(count)])
    given = lax.ppermute(keep, "seq", [(s, s + 1) for s in range(0, count, 2)])
    (out1,) = call(pair_kernel, [(slices, state_rows + ROWS, LANES)], "svv", 0.1, (place, keep, swapped))
    parities = [list(range(p, count, 2)) for p in range(2)]
    got1 = lax.all_to_all(
        out1, "seq", split_axis=0, concat_axis=0, axis_index_groups=parities, tiled=True
    )
    (block,) = call(
        query_kernel, [(tokens, feats + width + LANES)], "svvvvvv", 2.0,
        (place, queries, query_map[0], feat_k, values, given, swapped),
    )
    out2, prev_norm = call(
        functools.partial(forward_scan_kernel, state_rows),
        [(count, state_rows + block_rows * (width // LANES), LANES), (ROWS, LANES)],
        "ssvv", 0.1, (place, owner_ids, got1, blocks),
    )
    got2 = exchange(out2, "seq")
    grads, out3 = call(
        functools.partial(middle_kernel, block_rows, feats),
        [(tokens, width + LANES), (count, state_rows + ROWS, LANES)],
        "svvv", 1.0, (within, got2, prev_norm, block), [(tokens, width)],
    )
    got3 = exchange(out3, "seq")
    term_q, inner = call(
        weight_kernel, [(count, term_rows, LANES), (tokens, feats)], "svvvvvvvvv", 4.0,
        (place, queries, values, block, feat_k, got2, prev_norm, grads, given, swapped), [(tokens, half)],
    )
    out4, next_norm = call(
        functools.partial(backward_scan_kernel, state_rows),
        [(count, state_rows + term_rows, LANES), (ROWS, LANES)],
        "svv", 0.1, (place, got3, term_q),
    )
    got4 = exchange(out4, "seq")
    out5, grad_query = call(
        close_kernel, [(count, term_rows, LANES), (width // count, half)], "vvvvvv", 1.0,
        (keys, values, feat_k, inner, got4, next_norm),
    )
    got5 = exchange(out5, "seq")
    (grad_key,) = call(functools.partial(sum_kernel, 0), [(width // count, half)], "v", 0.1, (got5,))
    return (grad_query[None], grad_key[None])


def solution(mesh):
    placed = (
        P("seq", "head"),
        P("seq", "head"),
        P("seq", "head"),
        P(("seq", "head"), None),
        P("head", None, None),
        P("head", None, None),
        P(),
    )
    return jax.shard_map(
        per_device,
        mesh=mesh,
        in_specs=placed,
        out_specs=(P("head", "seq", None), P("head", "seq", None)),
        check_vma=False,
    )
```

```python
import functools

import jax
import jax.numpy as jnp
from jax import lax
from jax.experimental import pallas as pl
from jax.experimental.pallas import tpu as pltpu
from jax.sharding import PartitionSpec as P


exact_prec = lax.Precision.HIGHEST
LANES = 128
NORM_ROWS = 4
ROWS = 8
NN = (((1,), (0,)), ((), ()))
NT = (((1,), (1,)), ((), ()))
TN = (((0,), (0,)), ((), ()))


def halves(x):
    high = x.astype(jnp.bfloat16)
    return high, (x - high.astype(jnp.float32)).astype(jnp.bfloat16)


def dot3(a, b, dims):
    def one(x, y):
        return lax.dot_general(x, y, dims, preferred_element_type=jnp.float32)

    return one(a[0], b[0]) + (one(a[0], b[1]) + one(a[1], b[0]))


def features(rows, weights):
    pre = lax.dot_general(rows, weights, NN, precision=exact_prec, preferred_element_type=jnp.float32)
    first = jnp.exp(pre - jnp.max(pre, axis=-1, keepdims=True))
    second = jnp.exp(jnp.min(pre, axis=-1, keepdims=True) - pre)
    first = first / jnp.sum(first, axis=-1, keepdims=True)
    second = second / jnp.sum(second, axis=-1, keepdims=True)
    return first, second


def pack(out_ref, base, value):
    owners = out_ref.shape[0]
    for c in range(value.shape[1] // LANES):
        part = value[:, c * LANES : (c + 1) * LANES]
        out_ref[:, base + c * ROWS : base + (c + 1) * ROWS, :] = part.reshape(owners, ROWS, LANES)


def unpack(ref, base, count):
    owners = ref.shape[0]
    parts = [
        ref[:, base + c * ROWS : base + (c + 1) * ROWS, :].reshape(owners * ROWS, LANES)
        for c in range(count)
    ]
    return jnp.concatenate(parts, axis=-1)


def norm_tile(norm):
    count = norm.shape[1] // LANES
    rows = [norm[:, c * LANES : (c + 1) * LANES] for c in range(count)]
    rows.append(jnp.zeros((ROWS - count, LANES), jnp.float32))
    return jnp.concatenate(rows, axis=0)


def pack_norm(out_ref, base, norm):
    owners = out_ref.shape[0]
    tile = norm_tile(norm)
    out_ref[:, base : base + ROWS, :] = jnp.broadcast_to(tile[None], (owners, ROWS, LANES))


def key_kernel(place_ref, keys, weights, values, feat_ref, send_ref, keep_ref):
    half = weights.shape[1]
    first, second = features(keys[...], weights[...])
    feat_ref[:, :half] = first
    feat_ref[:, half:] = second
    feat = feat_ref[...]
    state = dot3(halves(values[...]), halves(feat), TN)
    split = state.shape[0] // 2
    odd = place_ref[0] % 2 == 1
    low, high = state[:split], state[split:]
    slices = split // ROWS
    norm = norm_tile(jnp.sum(feat, axis=0, keepdims=True))
    for ref, value in ((send_ref, jnp.where(odd, low, high)), (keep_ref, jnp.where(odd, high, low))):
        for c in range(value.shape[1] // LANES):
            part = value[:, c * LANES : (c + 1) * LANES]
            ref[:slices, c * ROWS : (c + 1) * ROWS, :] = part.reshape(slices, ROWS, LANES)
        ref[slices, :ROWS, :] = norm
        ref[slices, ROWS:, :] = jnp.zeros_like(ref[slices, ROWS:, :])


def pair_kernel(place_ref, keep_ref, got_ref, out_ref):
    slices, rows, _ = out_ref.shape
    rows -= ROWS
    odd = place_ref[0] % 2 == 1
    out_ref[:, :rows, :] = keep_ref[:slices] + got_ref[:slices]
    mine, other = keep_ref[slices, :NORM_ROWS, :], got_ref[slices, :NORM_ROWS, :]
    tile = jnp.concatenate([jnp.where(odd, other, mine), jnp.where(odd, mine, other)], axis=0)
    out_ref[:, rows:, :] = jnp.broadcast_to(tile[None], (slices, ROWS, LANES))


def unpack_half(ref):
    slices = ref.shape[0] - 1
    return jnp.concatenate(
        [
            ref[:slices, c * ROWS : (c + 1) * ROWS, :].reshape(slices * ROWS, LANES)
            for c in range(ref.shape[1] // ROWS)
        ],
        axis=-1,
    )


def even_state(place_ref, low_ref, high_ref):
    odd = place_ref[0] % 2 == 1
    both = jnp.concatenate([unpack_half(low_ref), unpack_half(high_ref)], axis=0)
    return jnp.where(odd, both, 0.0)


def unpack_pairs(ref, count):
    pairs = ref.shape[0] // 2
    halves_of = []
    for parity in range(2):
        parts = []
        for c in range(count):
            part = ref[:, c * ROWS : (c + 1) * ROWS, :].reshape(pairs, 2, ROWS, LANES)
            parts.append(part[:, parity].reshape(pairs * ROWS, LANES))
        halves_of.append(jnp.concatenate(parts, axis=-1))
    return jnp.concatenate(halves_of, axis=0)


def query_kernel(place_ref, queries, weights, feat_k, values, low_ref, high_ref, out_ref):
    half = weights.shape[1]
    tokens, width = queries.shape
    feats = 2 * half
    step = 256
    first, second = features(queries[...], weights[...])
    out_ref[:, :half] = first
    out_ref[:, half:feats] = second
    vals = halves(values[...])
    keys = halves(feat_k[...])
    before = halves(even_state(place_ref, low_ref, high_ref))
    for lo in range(0, tokens, step):
        hi = lo + step
        fq = halves(out_ref[lo:hi, :feats])
        scores = dot3(fq, (keys[0][:hi], keys[1][:hi]), NT)
        t = lax.broadcasted_iota(jnp.int32, scores.shape, 0) + lo
        s = lax.broadcasted_iota(jnp.int32, scores.shape, 1)
        scores = jnp.where(t >= s, scores, 0.0)
        raw = jnp.sum(scores, axis=-1, keepdims=True)
        out_ref[lo:hi, feats + width :] = jnp.broadcast_to(raw, (step, LANES))
        numer = dot3(halves(scores), (vals[0][:hi], vals[1][:hi]), NN)
        out_ref[lo:hi, feats : feats + width] = numer + dot3(fq, before, NT)


def owner_kernel(owner_ref, blocks_ref, out_ref):
    count, rows, width = blocks_ref.shape
    for place in range(count):
        owner = owner_ref[place]
        for c in range(width // LANES):
            out_ref[owner, c * rows : (c + 1) * rows, :] = blocks_ref[place, :, c * LANES : (c + 1) * LANES]


def forward_scan_kernel(state_rows, place_ref, got_ref, rest_ref, out_ref, norm_ref, sem):
    rest = pltpu.make_async_copy(rest_ref, out_ref.at[:, state_rows:, :], sem)
    rest.start()
    pairs = got_ref.shape[0]
    mine = place_ref[0] // 2
    odd = place_ref[0] % 2 == 1
    total = jnp.zeros((state_rows, LANES), jnp.float32)
    norm = jnp.zeros((NORM_ROWS, LANES), jnp.float32)
    for pair in range(pairs):
        out_ref[2 * pair, :state_rows, :] = total
        out_ref[2 * pair + 1, :state_rows, :] = total
        total = total + got_ref[pair, :state_rows, :]
        even = got_ref[pair, state_rows : state_rows + NORM_ROWS, :]
        last = got_ref[pair, state_rows + NORM_ROWS :, :]
        use_even = (pair < mine) | ((pair == mine) & odd)
        norm = norm + jnp.where(use_even, even, 0.0)
        norm = norm + jnp.where(pair < mine, last, 0.0)
    norm_ref[...] = jnp.concatenate([norm, jnp.zeros_like(norm)], axis=0)
    rest.wait()


def backward_scan_kernel(state_rows, place_ref, got_ref, rest_ref, out_ref, norm_ref, sem):
    rest = pltpu.make_async_copy(rest_ref, out_ref.at[:, state_rows:, :], sem)
    rest.start()
    mine = place_ref[0]
    total = jnp.zeros((state_rows, LANES), jnp.float32)
    norm = jnp.zeros((ROWS, LANES), jnp.float32)
    for place in range(got_ref.shape[0] - 1, -1, -1):
        out_ref[place, :state_rows, :] = total
        total = total + got_ref[place, :state_rows, :]
        norm = norm + jnp.where(place > mine, got_ref[place, state_rows:, :], 0.0)
    norm_ref[...] = norm
    rest.wait()


def norm_row(norm_ref, count):
    return jnp.concatenate([norm_ref[c : c + 1, :] for c in range(count)], axis=-1)


def middle_kernel(
    block_rows, feats, within_ref, got_ref, norm_ref, block_hbm, grad_hbm, out_ref,
    teacher_ref, block_ref, grad_ref, sems,
):
    fetch = pltpu.make_async_copy(block_hbm, block_ref, sems.at[0])
    fetch.start()
    width = teacher_ref.shape[1]
    count = got_ref.shape[0]
    chunks = feats // LANES
    state_rows = chunks * ROWS
    state = unpack_pairs(got_ref, chunks)
    for source in range(count):
        at = pl.multiple_of(within_ref[source] * block_rows, block_rows)
        for c in range(width // LANES):
            base = state_rows + c * block_rows
            teacher_ref[pl.ds(at, block_rows), c * LANES : (c + 1) * LANES] = got_ref[
                source, base : base + block_rows, :
            ]
    state = halves(state)
    fetch.wait()
    fq = block_ref[:, :feats]
    fq_pair = halves(fq)
    numerator = block_ref[:, feats : feats + width] + dot3(fq_pair, state, NT)
    prev_norm = norm_row(norm_ref, chunks)
    raw_sum = block_ref[:, feats + width : feats + width + 1] + jnp.sum(fq * prev_norm, axis=-1, keepdims=True)
    divisor = jnp.maximum(raw_sum, 1.0)
    student = numerator / divisor
    mismatch = student - teacher_ref[...]
    grad_num = mismatch / divisor
    grad_div = jnp.where(raw_sum > 1.0, -jnp.sum(mismatch * student, axis=-1, keepdims=True) / divisor, 0.0)
    grad_ref[:, :width] = grad_num
    grad_ref[:, width:] = jnp.broadcast_to(grad_div, (grad_div.shape[0], LANES))
    store = pltpu.make_async_copy(grad_ref, grad_hbm.at[0], sems.at[1])
    store.start()
    pack(out_ref, 0, dot3(halves(grad_num), fq_pair, TN))
    pack_norm(out_ref, state_rows, jnp.sum(grad_div * fq, axis=0, keepdims=True))
    store.wait()


def back_pair(feat, grad, half):
    first, second = feat[:, :half], feat[:, half:]
    grad_first, grad_second = grad[:, :half], grad[:, half:]
    lead = first * (grad_first - jnp.sum(first * grad_first, axis=-1, keepdims=True))
    trail = second * (grad_second - jnp.sum(second * grad_second, axis=-1, keepdims=True))
    return lead - trail


def weight_kernel(
    place_ref, queries, values, block_ref, feat_k, got_ref, norm_ref, grad_ref, low_ref, high_ref,
    term_ref, inner_ref, pre_ref,
):
    tokens, feats = feat_k.shape
    width = values.shape[1]
    half = feats // 2
    step = 256
    chunks = feats // LANES
    vals = halves(values[...])
    keys = halves(feat_k[...])
    states = halves(unpack_pairs(got_ref, chunks) + even_state(place_ref, low_ref, high_ref))
    prev_norm = norm_row(norm_ref, chunks)
    for lo in range(0, tokens, step):
        hi = lo + step
        div = grad_ref[lo:hi, width : width + 1]
        num = halves(grad_ref[lo:hi, :width])
        fq = block_ref[lo:hi, :feats]
        weights = dot3(num, (vals[0][:hi], vals[1][:hi]), NT) + div
        t = lax.broadcasted_iota(jnp.int32, weights.shape, 0) + lo
        s = lax.broadcasted_iota(jnp.int32, weights.shape, 1)
        weights = halves(jnp.where(t >= s, weights, 0.0))
        grad_fq = dot3(weights, (keys[0][:hi], keys[1][:hi]), NN) + dot3(num, states, NN) + div * prev_norm
        pre_ref[lo:hi, :] = back_pair(fq, grad_fq, half)
        part = dot3(weights, halves(fq), TN)
        if lo == 0:
            inner_ref[:hi, :] = part
        else:
            inner_ref[:lo, :] = inner_ref[:lo, :] + part[:lo]
            inner_ref[lo:hi, :] = part[lo:]
    pack(term_ref, 0, dot3(halves(queries[...]), halves(pre_ref[...]), TN))


def close_kernel(
    keys_hbm, values, feat_hbm, inner_hbm, got_ref, norm_ref, term_ref, query_ref, keys, feat_k, inner, sems
):
    pairs = ((inner_hbm, inner), (feat_hbm, feat_k), (keys_hbm, keys))
    fetches = [pltpu.make_async_copy(src, dst, sems.at[i]) for i, (src, dst) in enumerate(pairs)]
    for fetch in fetches:
        fetch.start()
    feats = feat_k.shape[1]
    chunks = feats // LANES
    state = unpack(got_ref, 0, chunks)
    grad_fk = dot3(halves(values[...]), halves(state), NN) + norm_row(norm_ref, chunks)
    sum_kernel(chunks * ROWS, got_ref, query_ref)
    fetches[0].wait()
    grad_fk = grad_fk + inner[...]
    fetches[1].wait()
    grad_pk = back_pair(feat_k[...], grad_fk, feats // 2)
    fetches[2].wait()
    pack(term_ref, 0, dot3(halves(keys[...]), halves(grad_pk), TN))


def sum_kernel(base, got_ref, out_ref):
    for c in range(out_ref.shape[1] // LANES):
        part = got_ref[:, base + c * ROWS : base + (c + 1) * ROWS, :]
        out_ref[:, c * LANES : (c + 1) * LANES] = jnp.sum(part, axis=0)


def call(body, outs, spaces, cost, args, scratch=(), sems=0, out_spaces=None, grant=24000):
    kinds = {"v": pltpu.VMEM, "s": pltpu.SMEM, "h": pltpu.HBM}
    return pl.pallas_call(
        body,
        out_shape=[jax.ShapeDtypeStruct(shape, jnp.float32) for shape in outs],
        in_specs=[pl.BlockSpec(memory_space=kinds[kind]) for kind in spaces],
        out_specs=[pl.BlockSpec(memory_space=kinds[kind]) for kind in out_spaces or "v" * len(outs)],
        scratch_shapes=[pltpu.VMEM(shape, jnp.float32) for shape in scratch]
        + ([pltpu.SemaphoreType.DMA((sems,))] if sems > 1 else [pltpu.SemaphoreType.DMA] * sems),
        compiler_params=pltpu.CompilerParams(vmem_limit_bytes=grant * 1024),
        cost_estimate=pl.CostEstimate(flops=int(cost * 1e9), bytes_accessed=1 << 20, transcendentals=0),
    )(*args)


def cut_kernel(in_ref, out_ref, sems):
    heads, _, width = out_ref.shape
    copies = [
        pltpu.make_async_copy(in_ref.at[:, pl.ds(h * width, width)], out_ref.at[h], sems.at[h])
        for h in range(heads)
    ]
    for copy in copies:
        copy.start()
    for copy in copies:
        copy.wait()


def cut_heads(rows, heads):
    count, total = rows.shape
    return pl.pallas_call(
        cut_kernel,
        out_shape=jax.ShapeDtypeStruct((heads, count, total // heads), rows.dtype),
        in_specs=[pl.BlockSpec(memory_space=pl.ANY)],
        out_specs=pl.BlockSpec(memory_space=pltpu.VMEM),
        scratch_shapes=[pltpu.SemaphoreType.DMA((heads,))],
        name="cut",
    )(rows)


def exchange(value, axis):
    return lax.all_to_all(value, axis, split_axis=0, concat_axis=0, tiled=True)


def per_device(queries, keys, values, teacher_out, query_map, key_map, block_map):
    tokens, width = queries.shape
    half = query_map.shape[2]
    feats = 2 * half
    count = lax.axis_size("seq")
    mine = lax.axis_index("seq")
    heads = lax.axis_size("head")
    chunks = feats // LANES
    state_rows = chunks * ROWS
    block_rows = tokens // count
    term_rows = half // LANES * ROWS

    place = mine.astype(jnp.int32).reshape(1)
    slot_ids = lax.dynamic_index_in_dim(block_map, mine, 0, keepdims=False)
    owner_ids = slot_ids // count
    within = jnp.sum(jnp.where(block_map // count == mine, block_map % count, 0), axis=1).astype(jnp.int32)
    gathered = exchange(cut_heads(teacher_out, heads), "head")
    blocks = gathered.reshape(count, block_rows, width)

    slices = count // 2
    half_shape = (slices + 1, state_rows, LANES)
    feat_k, send, keep = call(
        key_kernel, [(tokens, feats), half_shape, half_shape], "svvv", 1.0,
        (place, keys, key_map[0], values),
    )
    swapped = lax.ppermute(send, "seq", [(s, s ^ 1) for s in range(count)])
    given = lax.ppermute(keep, "seq", [(s, s + 1) for s in range(0, count, 2)])
    (out1,) = call(pair_kernel, [(slices, state_rows + ROWS, LANES)], "svv", 0.1, (place, keep, swapped))
    parities = [list(range(p, count, 2)) for p in range(2)]
    got1 = lax.all_to_all(
        out1, "seq", split_axis=0, concat_axis=0, axis_index_groups=parities, tiled=True
    )
    (block,) = call(
        query_kernel, [(tokens, feats + width + LANES)], "svvvvvv", 2.0,
        (place, queries, query_map[0], feat_k, values, given, swapped),
    )
    teacher_rows = block_rows * (width // LANES)
    (placed,) = call(owner_kernel, [(count, teacher_rows, LANES)], "sv", 1.0, (owner_ids, blocks))
    out2, prev_norm = call(
        functools.partial(forward_scan_kernel, state_rows),
        [(count, state_rows + teacher_rows, LANES), (ROWS, LANES)],
        "svh", 0.1, (place, got1, placed), sems=1, grant=54500,
    )
    got2 = exchange(out2, "seq")
    grads, out3 = call(
        functools.partial(middle_kernel, block_rows, feats),
        [(3, tokens, width + LANES), (count, state_rows + ROWS, LANES)],
        "svvh", 1.0, (within, got2, prev_norm, block),
        [(tokens, width), (tokens, feats + width + LANES), (tokens, width + LANES)], 2, "hv", 52000,
    )
    got3 = exchange(out3, "seq")
    grads = grads[0]
    term_q, inner = call(
        weight_kernel, [(count, term_rows, LANES), (tokens, feats)], "svvvvvvvvv", 4.0,
        (place, queries, values, block, feat_k, got2, prev_norm, grads, given, swapped), [(tokens, half)],
    )
    out4, next_norm = call(
        functools.partial(backward_scan_kernel, state_rows),
        [(count, state_rows + term_rows, LANES), (ROWS, LANES)],
        "svh", 0.1, (place, got3, term_q), sems=1, grant=54500,
    )
    got4 = exchange(out4, "seq")
    out5, grad_query = call(
        close_kernel, [(count, term_rows, LANES), (width // count, half)], "hvhhvv", 1.0,
        (keys, values, feat_k, inner, got4, next_norm),
        [(tokens, width), (tokens, feats), (tokens, feats)], 3, grant=54500,
    )
    got5 = exchange(out5, "seq")
    (grad_key,) = call(functools.partial(sum_kernel, 0), [(width // count, half)], "v", 0.1, (got5,))
    return (grad_query[None], grad_key[None])


def solution(mesh):
    placed = (
        P("seq", "head"),
        P("seq", "head"),
        P("seq", "head"),
        P(("seq", "head"), None),
        P("head", None, None),
        P("head", None, None),
        P(),
    )
    return jax.shard_map(
        per_device,
        mesh=mesh,
        in_specs=placed,
        out_specs=(P("head", "seq", None), P("head", "seq", None)),
        check_vma=False,
    )
```

```python
import functools

import jax
import jax.numpy as jnp
from jax import lax
from jax.experimental import pallas as pl
from jax.experimental.pallas import tpu as pltpu
from jax.sharding import PartitionSpec as P


exact_prec = lax.Precision.HIGHEST
LANES = 128
NORM_ROWS = 4
ROWS = 8
NN = (((1,), (0,)), ((), ()))
NT = (((1,), (1,)), ((), ()))
TN = (((0,), (0,)), ((), ()))


def halves(x):
    high = x.astype(jnp.bfloat16)
    return high, (x - high.astype(jnp.float32)).astype(jnp.bfloat16)


def dot3(a, b, dims):
    def one(x, y):
        return lax.dot_general(x, y, dims, preferred_element_type=jnp.float32)

    return one(a[0], b[0]) + (one(a[0], b[1]) + one(a[1], b[0]))


def features(rows, weights):
    pre = lax.dot_general(rows, weights, NN, precision=exact_prec, preferred_element_type=jnp.float32)
    first = jnp.exp(pre - jnp.max(pre, axis=-1, keepdims=True))
    second = jnp.exp(jnp.min(pre, axis=-1, keepdims=True) - pre)
    first = first / jnp.sum(first, axis=-1, keepdims=True)
    second = second / jnp.sum(second, axis=-1, keepdims=True)
    return first, second


def pack(out_ref, base, value):
    owners = out_ref.shape[0]
    for c in range(value.shape[1] // LANES):
        part = value[:, c * LANES : (c + 1) * LANES]
        out_ref[:, base + c * ROWS : base + (c + 1) * ROWS, :] = part.reshape(owners, ROWS, LANES)


def unpack(ref, base, count):
    owners = ref.shape[0]
    parts = [
        ref[:, base + c * ROWS : base + (c + 1) * ROWS, :].reshape(owners * ROWS, LANES)
        for c in range(count)
    ]
    return jnp.concatenate(parts, axis=-1)


def norm_tile(norm):
    count = norm.shape[1] // LANES
    rows = [norm[:, c * LANES : (c + 1) * LANES] for c in range(count)]
    rows.append(jnp.zeros((ROWS - count, LANES), jnp.float32))
    return jnp.concatenate(rows, axis=0)


def pack_norm(out_ref, base, norm):
    owners = out_ref.shape[0]
    tile = norm_tile(norm)
    out_ref[:, base : base + ROWS, :] = jnp.broadcast_to(tile[None], (owners, ROWS, LANES))


def key_kernel(place_ref, keys, weights, values, feat_ref, send_ref, keep_ref):
    half = weights.shape[1]
    first, second = features(keys[...], weights[...])
    feat_ref[:, :half] = first
    feat_ref[:, half:] = second
    feat = feat_ref[...]
    state = dot3(halves(values[...]), halves(feat), TN)
    split = state.shape[0] // 2
    odd = place_ref[0] % 2 == 1
    low, high = state[:split], state[split:]
    slices = split // ROWS
    norm = norm_tile(jnp.sum(feat, axis=0, keepdims=True))
    for ref, value in ((send_ref, jnp.where(odd, low, high)), (keep_ref, jnp.where(odd, high, low))):
        for c in range(value.shape[1] // LANES):
            part = value[:, c * LANES : (c + 1) * LANES]
            ref[:slices, c * ROWS : (c + 1) * ROWS, :] = part.reshape(slices, ROWS, LANES)
        ref[slices, :ROWS, :] = norm
        ref[slices, ROWS:, :] = jnp.zeros_like(ref[slices, ROWS:, :])


def pair_kernel(place_ref, keep_ref, got_ref, out_ref):
    slices, rows, _ = out_ref.shape
    rows -= ROWS
    odd = place_ref[0] % 2 == 1
    out_ref[:, :rows, :] = keep_ref[:slices] + got_ref[:slices]
    mine, other = keep_ref[slices, :NORM_ROWS, :], got_ref[slices, :NORM_ROWS, :]
    tile = jnp.concatenate([jnp.where(odd, other, mine), jnp.where(odd, mine, other)], axis=0)
    out_ref[:, rows:, :] = jnp.broadcast_to(tile[None], (slices, ROWS, LANES))


def unpack_half(ref):
    slices = ref.shape[0] - 1
    return jnp.concatenate(
        [
            ref[:slices, c * ROWS : (c + 1) * ROWS, :].reshape(slices * ROWS, LANES)
            for c in range(ref.shape[1] // ROWS)
        ],
        axis=-1,
    )


def even_state(place_ref, low_ref, high_ref):
    odd = place_ref[0] % 2 == 1
    both = jnp.concatenate([unpack_half(low_ref), unpack_half(high_ref)], axis=0)
    return jnp.where(odd, both, 0.0)


def unpack_pairs(ref, count):
    pairs = ref.shape[0] // 2
    halves_of = []
    for parity in range(2):
        parts = []
        for c in range(count):
            part = ref[:, c * ROWS : (c + 1) * ROWS, :].reshape(pairs, 2, ROWS, LANES)
            parts.append(part[:, parity].reshape(pairs * ROWS, LANES))
        halves_of.append(jnp.concatenate(parts, axis=-1))
    return jnp.concatenate(halves_of, axis=0)


def query_kernel(place_ref, queries, weights, feat_k, values, low_ref, high_ref, out_ref):
    half = weights.shape[1]
    tokens, width = queries.shape
    feats = 2 * half
    step = 256
    first, second = features(queries[...], weights[...])
    out_ref[:, :half] = first
    out_ref[:, half:feats] = second
    vals = halves(values[...])
    keys = halves(feat_k[...])
    before = halves(even_state(place_ref, low_ref, high_ref))
    for lo in range(0, tokens, step):
        hi = lo + step
        fq = halves(out_ref[lo:hi, :feats])
        scores = dot3(fq, (keys[0][:hi], keys[1][:hi]), NT)
        t = lax.broadcasted_iota(jnp.int32, scores.shape, 0) + lo
        s = lax.broadcasted_iota(jnp.int32, scores.shape, 1)
        scores = jnp.where(t >= s, scores, 0.0)
        raw = jnp.sum(scores, axis=-1, keepdims=True)
        out_ref[lo:hi, feats + width :] = jnp.broadcast_to(raw, (step, LANES))
        numer = dot3(halves(scores), (vals[0][:hi], vals[1][:hi]), NN)
        out_ref[lo:hi, feats : feats + width] = numer + dot3(fq, before, NT)


def forward_scan_kernel(state_rows, place_ref, owner_ref, got_ref, blocks_ref, out_ref, norm_ref):
    pairs = got_ref.shape[0]
    mine = place_ref[0] // 2
    odd = place_ref[0] % 2 == 1
    total = jnp.zeros((state_rows, LANES), jnp.float32)
    norm = jnp.zeros((NORM_ROWS, LANES), jnp.float32)
    for pair in range(pairs):
        out_ref[2 * pair, :state_rows, :] = total
        out_ref[2 * pair + 1, :state_rows, :] = total
        total = total + got_ref[pair, :state_rows, :]
        even = got_ref[pair, state_rows : state_rows + NORM_ROWS, :]
        last = got_ref[pair, state_rows + NORM_ROWS :, :]
        use_even = (pair < mine) | ((pair == mine) & odd)
        norm = norm + jnp.where(use_even, even, 0.0)
        norm = norm + jnp.where(pair < mine, last, 0.0)
    norm_ref[...] = jnp.concatenate([norm, jnp.zeros_like(norm)], axis=0)
    count, rows, width = blocks_ref.shape
    for place in range(count):
        owner = owner_ref[place]
        for c in range(width // LANES):
            base = state_rows + c * rows
            out_ref[owner, base : base + rows, :] = blocks_ref[place, :, c * LANES : (c + 1) * LANES]


def backward_scan_kernel(state_rows, place_ref, got_ref, out_ref, norm_ref):
    mine = place_ref[0]
    total = jnp.zeros((state_rows, LANES), jnp.float32)
    norm = jnp.zeros((ROWS, LANES), jnp.float32)
    for place in range(got_ref.shape[0] - 1, -1, -1):
        out_ref[place, :state_rows, :] = total
        total = total + got_ref[place, :state_rows, :]
        norm = norm + jnp.where(place > mine, got_ref[place, state_rows:, :], 0.0)
    norm_ref[...] = norm


def norm_row(norm_ref, count):
    return jnp.concatenate([norm_ref[c : c + 1, :] for c in range(count)], axis=-1)


def middle_kernel(
    block_rows, feats, within_ref, got_ref, norm_ref, block_ref, grad_ref, out_ref, teacher_ref
):
    width = teacher_ref.shape[1]
    count = got_ref.shape[0]
    chunks = feats // LANES
    state_rows = chunks * ROWS
    state = unpack_pairs(got_ref, chunks)
    for source in range(count):
        at = pl.multiple_of(within_ref[source] * block_rows, block_rows)
        for c in range(width // LANES):
            base = state_rows + c * block_rows
            teacher_ref[pl.ds(at, block_rows), c * LANES : (c + 1) * LANES] = got_ref[
                source, base : base + block_rows, :
            ]
    fq = block_ref[:, :feats]
    fq_pair = halves(fq)
    numerator = block_ref[:, feats : feats + width] + dot3(fq_pair, halves(state), NT)
    prev_norm = norm_row(norm_ref, chunks)
    raw_sum = block_ref[:, feats + width : feats + width + 1] + jnp.sum(fq * prev_norm, axis=-1, keepdims=True)
    divisor = jnp.maximum(raw_sum, 1.0)
    student = numerator / divisor
    mismatch = student - teacher_ref[...]
    grad_num = mismatch / divisor
    grad_div = jnp.where(raw_sum > 1.0, -jnp.sum(mismatch * student, axis=-1, keepdims=True) / divisor, 0.0)
    grad_ref[:, :width] = grad_num
    grad_ref[:, width:] = jnp.broadcast_to(grad_div, (grad_div.shape[0], LANES))
    pack(out_ref, 0, dot3(halves(grad_num), fq_pair, TN))
    pack_norm(out_ref, state_rows, jnp.sum(grad_div * fq, axis=0, keepdims=True))


def back_pair(feat, grad, half):
    first, second = feat[:, :half], feat[:, half:]
    grad_first, grad_second = grad[:, :half], grad[:, half:]
    lead = first * (grad_first - jnp.sum(first * grad_first, axis=-1, keepdims=True))
    trail = second * (grad_second - jnp.sum(second * grad_second, axis=-1, keepdims=True))
    return lead - trail


def weight_kernel(
    place_ref, queries, values, block_ref, feat_k, got_ref, norm_ref, grad_ref, low_ref, high_ref,
    term_ref, inner_ref, pre_ref,
):
    tokens, feats = feat_k.shape
    width = values.shape[1]
    half = feats // 2
    step = 256
    chunks = feats // LANES
    vals = halves(values[...])
    keys = halves(feat_k[...])
    states = halves(unpack_pairs(got_ref, chunks) + even_state(place_ref, low_ref, high_ref))
    prev_norm = norm_row(norm_ref, chunks)
    for lo in range(0, tokens, step):
        hi = lo + step
        div = grad_ref[lo:hi, width : width + 1]
        num = halves(grad_ref[lo:hi, :width])
        fq = block_ref[lo:hi, :feats]
        weights = dot3(num, (vals[0][:hi], vals[1][:hi]), NT) + div
        t = lax.broadcasted_iota(jnp.int32, weights.shape, 0) + lo
        s = lax.broadcasted_iota(jnp.int32, weights.shape, 1)
        weights = halves(jnp.where(t >= s, weights, 0.0))
        grad_fq = dot3(weights, (keys[0][:hi], keys[1][:hi]), NN) + dot3(num, states, NN) + div * prev_norm
        pre_ref[lo:hi, :] = back_pair(fq, grad_fq, half)
        part = dot3(weights, halves(fq), TN)
        if lo == 0:
            inner_ref[:hi, :] = part
        else:
            inner_ref[:lo, :] = inner_ref[:lo, :] + part[:lo]
            inner_ref[lo:hi, :] = part[lo:]
    pack(term_ref, 0, dot3(halves(queries[...]), halves(pre_ref[...]), TN))


def close_kernel(keys, values, feat_k, inner, got_ref, norm_ref, query_ref, term_ref):
    feats = feat_k.shape[1]
    chunks = feats // LANES
    state = unpack(got_ref, 0, chunks)
    grad_fk = inner[...] + dot3(halves(values[...]), halves(state), NN) + norm_row(norm_ref, chunks)
    grad_pk = back_pair(feat_k[...], grad_fk, feats // 2)
    pack(term_ref, 0, dot3(halves(keys[...]), halves(grad_pk), TN))
    term_ref[:, query_ref.shape[1] :, :] = query_ref[...]


def sum_kernel(got_ref, key_ref, query_ref):
    sum_slices(0, got_ref, key_ref)
    sum_slices(got_ref.shape[1] // 2, got_ref, query_ref)


def sum_slices(base, got_ref, out_ref):
    for c in range(out_ref.shape[1] // LANES):
        part = got_ref[:, base + c * ROWS : base + (c + 1) * ROWS, :]
        out_ref[:, c * LANES : (c + 1) * LANES] = jnp.sum(part, axis=0)


def call(body, outs, spaces, cost, args, scratch=()):
    vmem = pl.BlockSpec(memory_space=pltpu.VMEM)
    smem = pl.BlockSpec(memory_space=pltpu.SMEM)
    return pl.pallas_call(
        body,
        out_shape=[jax.ShapeDtypeStruct(shape, jnp.float32) for shape in outs],
        in_specs=[smem if kind == "s" else vmem for kind in spaces],
        out_specs=[vmem] * len(outs),
        scratch_shapes=[pltpu.VMEM(shape, jnp.float32) for shape in scratch],
        compiler_params=pltpu.CompilerParams(vmem_limit_bytes=24 * 1024 * 1024),
        cost_estimate=pl.CostEstimate(flops=int(cost * 1e9), bytes_accessed=1 << 20, transcendentals=0),
    )(*args)


def cut_kernel(in_ref, out_ref, sems):
    heads, _, width = out_ref.shape
    copies = [
        pltpu.make_async_copy(in_ref.at[:, pl.ds(h * width, width)], out_ref.at[h], sems.at[h])
        for h in range(heads)
    ]
    for copy in copies:
        copy.start()
    for copy in copies:
        copy.wait()


def cut_heads(rows, heads):
    count, total = rows.shape
    return pl.pallas_call(
        cut_kernel,
        out_shape=jax.ShapeDtypeStruct((heads, count, total // heads), rows.dtype),
        in_specs=[pl.BlockSpec(memory_space=pl.ANY)],
        out_specs=pl.BlockSpec(memory_space=pltpu.VMEM),
        scratch_shapes=[pltpu.SemaphoreType.DMA((heads,))],
        name="cut",
    )(rows)


def exchange(value, axis):
    return lax.all_to_all(value, axis, split_axis=0, concat_axis=0, tiled=True)


def per_device(queries, keys, values, teacher_out, query_map, key_map, block_map):
    tokens, width = queries.shape
    half = query_map.shape[2]
    feats = 2 * half
    count = lax.axis_size("seq")
    mine = lax.axis_index("seq")
    heads = lax.axis_size("head")
    chunks = feats // LANES
    state_rows = chunks * ROWS
    block_rows = tokens // count
    term_rows = half // LANES * ROWS

    place = mine.astype(jnp.int32).reshape(1)
    slot_ids = lax.dynamic_index_in_dim(block_map, mine, 0, keepdims=False)
    owner_ids = slot_ids // count
    within = jnp.sum(jnp.where(block_map // count == mine, block_map % count, 0), axis=1).astype(jnp.int32)
    gathered = exchange(cut_heads(teacher_out, heads), "head")
    blocks = gathered.reshape(count, block_rows, width)

    slices = count // 2
    half_shape = (slices + 1, state_rows, LANES)
    feat_k, send, keep = call(
        key_kernel, [(tokens, feats), half_shape, half_shape], "svvv", 1.0,
        (place, keys, key_map[0], values),
    )
    swapped = lax.ppermute(send, "seq", [(s, s ^ 1) for s in range(count)])
    given = lax.ppermute(keep, "seq", [(s, s + 1) for s in range(0, count, 2)])
    (out1,) = call(pair_kernel, [(slices, state_rows + ROWS, LANES)], "svv", 0.1, (place, keep, swapped))
    parities = [list(range(p, count, 2)) for p in range(2)]
    got1 = lax.all_to_all(
        out1, "seq", split_axis=0, concat_axis=0, axis_index_groups=parities, tiled=True
    )
    (block,) = call(
        query_kernel, [(tokens, feats + width + LANES)], "svvvvvv", 2.0,
        (place, queries, query_map[0], feat_k, values, given, swapped),
    )
    out2, prev_norm = call(
        functools.partial(forward_scan_kernel, state_rows),
        [(count, state_rows + block_rows * (width // LANES), LANES), (ROWS, LANES)],
        "ssvv", 0.1, (place, owner_ids, got1, blocks),
    )
    got2 = exchange(out2, "seq")
    grads, out3 = call(
        functools.partial(middle_kernel, block_rows, feats),
        [(tokens, width + LANES), (count, state_rows + ROWS, LANES)],
        "svvv", 1.0, (within, got2, prev_norm, block), [(tokens, width)],
    )
    got3 = exchange(out3, "seq")
    term_q, inner = call(
        weight_kernel, [(count, term_rows, LANES), (tokens, feats)], "svvvvvvvvv", 4.0,
        (place, queries, values, block, feat_k, got2, prev_norm, grads, given, swapped), [(tokens, half)],
    )
    out4, next_norm = call(
        functools.partial(backward_scan_kernel, state_rows),
        [(count, state_rows, LANES), (ROWS, LANES)],
        "sv", 0.1, (place, got3),
    )
    got4 = exchange(out4, "seq")
    (out5,) = call(
        close_kernel, [(count, 2 * term_rows, LANES)], "vvvvvvv", 1.0,
        (keys, values, feat_k, inner, got4, next_norm, term_q),
    )
    got5 = exchange(out5, "seq")
    grad_key, grad_query = call(sum_kernel, [(width // count, half)] * 2, "v", 0.1, (got5,))
    return (grad_query[None], grad_key[None])


def solution(mesh):
    placed = (
        P("seq", "head"),
        P("seq", "head"),
        P("seq", "head"),
        P(("seq", "head"), None),
        P("head", None, None),
        P("head", None, None),
        P(),
    )
    return jax.shard_map(
        per_device,
        mesh=mesh,
        in_specs=placed,
        out_specs=(P("head", "seq", None), P("head", "seq", None)),
        check_vma=False,
    )
```
